32 devices in a mesh: row: 4 (over z), col: 4 (over y, core), img: 2 (over x).
Axes of the slice: x: 2, y: 2, z: 4, core: 2. Of those that a mesh axis runs over, the one named last changes fastest.
Arguments:
- latent: bfloat16 [2, 4, 128, 128], P('img', None, 'row', 'col'), may hold values from -6 to 6
- context: bfloat16 [40, 1152], P('img'), may hold values from -6 to 6
- segment: int32 [2, 64, 64], P('img'), may hold values from -1 to 19, as said below
- patch_weight: bfloat16 [16, 1152], replicated, may hold values from -1.5 to 1.5
- patch_bias: bfloat16 [1152], replicated, may hold values from -4 to 4
- adaln_weight: bfloat16 [1152, 6912], replicated, may hold values from -0.1875 to 0.1875
- adaln_bias: bfloat16 [6912], replicated, may hold values from -6 to 6
- heads_weight: bfloat16 [1152, 3456], replicated, may hold values from -0.1875 to 0.1875
- query_bias: bfloat16 [1152], replicated, may hold values from -4 to 4
- value_bias: bfloat16 [1152], replicated, may hold values from -1.5 to 1.5
- merge_weight: bfloat16 [1152, 1152], replicated, may hold values from -1 to 1
- merge_bias: bfloat16 [1152], replicated, may hold values from -4 to 4
- up_weight: bfloat16 [1152, 4608], replicated, may hold values from -0.1875 to 0.1875
- up_bias: bfloat16 [4608], replicated, may hold values from -4 to 4
- down_weight: bfloat16 [4608, 1152], replicated, may hold values from -0.09375 to 0.09375
- down_bias: bfloat16 [1152], replicated, may hold values from -6 to 6
- final_weight: bfloat16 [1152, 16], replicated, may hold values from -0.1875 to 0.1875
- final_bias: bfloat16 [16], replicated, may hold values from -4 to 4
- cotangent: bfloat16 [2, 4, 128, 128], P('img', None, 'row', 'col'), may hold values from -6 to 6
Outputs:
- output: float32 [2, 4, 128, 128], P('img', None, 'row', 'col')
- latent_gradient: float32 [2, 4, 128, 128], P('img', None, 'row', 'col')
- context_gradient: float32 [40, 1152], P('img')
- patch_weight_grad: float32 [16, 1152], replicated
- patch_bias_grad: float32 [1152], replicated
- adaln_weight_grad: float32 [1152, 6912], P(('row', 'col'), 'img')
- adaln_bias_grad: float32 [6912], replicated
- heads_weight_grad: float32 [1152, 3456], P(('row', 'col'), 'img')
- query_bias_grad: float32 [1152], replicated
- value_bias_grad: float32 [1152], replicated
- merge_weight_grad: float32 [1152, 1152], P(('row', 'col'), 'img')
- merge_bias_grad: float32 [1152], replicated
- up_weight_grad: float32 [1152, 4608], P(('row', 'col'), 'img')
- up_bias_grad: float32 [4608], replicated
- down_weight_grad: float32 [4608, 1152], P(('row', 'col'), 'img')
- down_bias_grad: float32 [1152], replicated
- final_weight_grad: float32 [1152, 16], replicated
- final_bias_grad: float32 [16], replicated
The draws below stay inside these ranges and needn't reach their ends.
Inputs may be any that keep to these rules, and one draw needn't show every extreme that they name: `segment`: each canvas is cut into aligned blocks of 32 x 32 patches, numbered b row by row; a block holds either one image whose id is 5b + 4 on all its patches, or four images of 16 x 32/2 patches with ids 5b + q, q = 2 (lower half) + (right half), each of which may be padding with id -1.
All inputs are finite; a program needn't handle non-finite values.
Results may differ from the reference program's by a relative error of at most 0.025.
Values may be sent and summed in bfloat16 or wider, within the bound.
A program may use at most 256 MiB of HBM per device.

```python
import math
import jax
import jax.numpy as jnp
from jax import lax

D = 1152
FF = 4608
HEADS = 16
HEAD = 72
CHANNELS = 4
BLOCK = 32
PROWS = 64
PCOLS = 64
NBR = 2
NBC = 2
SLOTS = 20
GROUPS = 2


def draw_segment(key, part):
    kind_key = jax.random.fold_in(key, 11)
    live_key = jax.random.fold_in(key, 23)
    kinds = jax.random.randint(kind_key, (GROUPS, NBR, NBC), 0, 2)
    kinds = kinds.at[0, NBR - 1, NBC - 1].set(1)
    kinds = kinds.at[0, 0, 0].set(0)
    lives = jax.random.randint(live_key, (GROUPS, NBR, NBC, 4), 0, 12) != 0
    lives = lives.at[0, 0, 0, 3].set(False)
    grid_rows = jnp.arange(PROWS, dtype=jnp.int32)[:, None]
    grid_cols = jnp.arange(PCOLS, dtype=jnp.int32)[None, :]
    block_row = grid_rows // BLOCK
    block_col = grid_cols // BLOCK
    quarter = grid_rows % BLOCK // (BLOCK // 2) * 2 + grid_cols % BLOCK // (BLOCK // 2)
    block_ids = block_row * NBC + block_col
    kind_map = kinds[:, block_row, block_col]
    live_map = lives[:, block_row, block_col, quarter]
    small_ids = jnp.where(live_map, 5 * block_ids + quarter, -1)
    return jnp.where(kind_map == 1, 5 * block_ids + 4, small_ids).astype(jnp.int32)


def level_of(rng, shape, shards, smallest, top_value):
    def one(axis_at, blocks):
        draws = jax.random.uniform(jax.random.fold_in(jax.random.fold_in(rng, 6), axis_at), (blocks,), jnp.float32, smallest / len(shards), top_value / len(shards))
        return jnp.repeat(jnp.exp(draws), shape[axis_at] // blocks).reshape((-1,) + (1,) * (len(shape) - axis_at - 1))

    loudness = one(*shards[0])
    for cut in shards[1:]:
        loudness = loudness * one(*cut)
    return loudness


def normal_values(key, extent, spread, reach, shards=(), kind=jnp.bfloat16):
    drawn = jax.random.normal(key, extent, jnp.float32) * spread
    if len(shards) > 0:
        drawn = level_of(key, extent, shards, -0.22, 0.18) * drawn
    return jnp.clip(drawn, min=-reach, max=reach).astype(kind)


def setup_inputs(seed: int = 0) -> dict:
    streams_of = jax.random.split(jax.random.key(seed), 20)
    return {
        "latent": normal_values(streams_of[0], (GROUPS, CHANNELS, 2 * PROWS, 2 * PCOLS), 1.0, 6.0, ((0, 2), (2, 4), (3, 4))),
        "context": normal_values(streams_of[1], (GROUPS * SLOTS, D), 1.0, 6.0, ((0, 2),)),
        "segment": draw_segment(jax.random.fold_in(streams_of[19], 71), 0),
        "patch_weight": normal_values(streams_of[3], (4 * CHANNELS, D), (4 * CHANNELS) ** -0.5, 1.5),
        "patch_bias": normal_values(streams_of[4], (D,), 0.3, 4.0),
        "adaln_weight": normal_values(streams_of[5], (D, 6 * D), D ** -0.5, 0.1875),
        "adaln_bias": normal_values(streams_of[6], (6 * D,), 0.5, 6.0),
        "heads_weight": normal_values(streams_of[7], (D, 3 * D), D ** -0.5, 0.1875),
        "query_bias": normal_values(streams_of[8], (D,), 0.3, 4.0),
        "value_bias": normal_values(streams_of[9], (D,), 0.1, 1.5),
        "merge_weight": normal_values(streams_of[10], (D, D), (D // 32) ** -0.5, 1.0),
        "merge_bias": normal_values(streams_of[11], (D,), 0.3, 4.0),
        "up_weight": normal_values(streams_of[12], (D, FF), D ** -0.5, 0.1875),
        "up_bias": normal_values(streams_of[13], (FF,), 0.3, 4.0),
        "down_weight": normal_values(streams_of[14], (FF, D), FF ** -0.5, 0.09375),
        "down_bias": normal_values(streams_of[15], (D,), 0.6, 6.0),
        "final_weight": normal_values(streams_of[16], (D, 4 * CHANNELS), D ** -0.5, 0.1875),
        "final_bias": normal_values(streams_of[17], (4 * CHANNELS,), 0.3, 4.0),
        "cotangent": normal_values(streams_of[18], (GROUPS, CHANNELS, 2 * PROWS, 2 * PCOLS), 1.0, 6.0, ((0, 2), (2, 4), (3, 4))),
    }


@jax.custom_vjp
def low(v):
    return lax.optimization_barrier(v.astype(jnp.bfloat16)).astype(jnp.float32)

@jax.custom_vjp
def low_back(v):
    return v

def low_keep(v):
    return (low(v), None)

def low_pass(kept, grad):
    return (grad,)

def back_keep(v):
    return (v, None)

def back_low(kept, grad):
    return (low(grad),)
low.defvjp(low_keep, low_pass)
low_back.defvjp(back_keep, back_low)
MASKED = -1e+30
EPSILON = 1e-06

def product(left_side, right_side):
    return jnp.dot(left_side, right_side, precision=lax.Precision.HIGHEST, preferred_element_type=jnp.float32)

def layer_norm(tensor):
    center = tensor - lax.optimization_barrier(jnp.mean(tensor, axis=-1, keepdims=True))
    return center * lax.rsqrt(lax.optimization_barrier(jnp.mean(center * center, axis=-1, keepdims=True)) + EPSILON)

def position_table(segments, grid_rows, grid_cols):
    quarter = D // 4
    is_large = segments % 5 == 4
    patch_row = jnp.where(is_large, grid_rows % BLOCK, grid_rows % (BLOCK // 2)).astype(jnp.float32)
    patch_col = jnp.where(is_large, grid_cols % BLOCK, grid_cols % (BLOCK // 2)).astype(jnp.float32)
    frequency = 1.0 / 10000.0 ** (jnp.arange(quarter, dtype=jnp.float32) / quarter)
    angle_r = patch_row[:, None] * frequency[None, :]
    angle_c = patch_col[:, None] * frequency[None, :]
    return jnp.concatenate([jnp.sin(angle_r), jnp.cos(angle_r), jnp.sin(angle_c), jnp.cos(angle_c)], axis=1)

def attend(queries, keys, values, seg_flat):
    tok_count = queries.shape[0]
    block_rows = 512
    block_count = tok_count // block_rows
    keys_h = keys.reshape(tok_count, HEADS, HEAD)
    values_h = values.reshape(tok_count, HEADS, HEAD)
    score_scale = 1.0 / math.sqrt(HEAD)

    def query_block(inputs):
        query_blk, seg_blk = inputs
        scores = jnp.einsum('qhd,khd->hqk', query_blk, keys_h, precision=lax.Precision.HIGHEST) * score_scale
        allowed = (seg_blk[:, None] == seg_flat[None, :])[None]
        scores = low_back(jnp.where(allowed, scores, MASKED))
        running_max = lax.optimization_barrier(jnp.max(scores, axis=-1, keepdims=True))
        expo = jnp.exp(scores - running_max)
        probability = low(expo / lax.optimization_barrier(jnp.sum(expo, axis=-1, keepdims=True)))
        result = jnp.einsum('hqk,khd->qhd', probability, values_h, precision=lax.Precision.HIGHEST)
        return result.reshape(block_rows, D)
    outs = lax.map(jax.checkpoint(query_block), (queries.reshape(block_count, block_rows, HEADS, HEAD), seg_flat.reshape(block_count, block_rows)))
    return outs.reshape(tok_count, D)

def group_forward(params, latent_g, context_g, segment_g):
    patch_weight, patch_bias, adaln_weight, adaln_bias, heads_weight, query_bias, value_bias, merge_weight, merge_bias, up_weight, up_bias, down_weight, down_bias, final_weight, final_bias = params
    canvas = jnp.roll(latent_g, (1, 1), axis=(1, 2))
    height = canvas.shape[1] // 2
    breadth = canvas.shape[2] // 2
    tok_count = height * breadth
    patches = canvas.reshape(CHANNELS, height, 2, breadth, 2).transpose(1, 3, 0, 2, 4).reshape(tok_count, CHANNELS * 4)
    seg_flat = segment_g.reshape(tok_count)
    token_ids = jnp.arange(tok_count, dtype=jnp.int32)
    live_mask = (seg_flat >= 0).astype(jnp.float32)
    embedded = low_back(product(patches, patch_weight)) + patch_bias + position_table(seg_flat, token_ids // breadth, token_ids % breadth)
    context_low = low(jax.nn.silu(context_g))
    modulation = low_back(product(context_low, adaln_weight) + adaln_bias)
    onehot = (seg_flat[:, None] == jnp.arange(SLOTS, dtype=jnp.int32)[None, :]).astype(jnp.float32)
    per_token = product(onehot, modulation)
    shift_a, scale_a, gate_a, shift_b, scale_b, gate_b = jnp.split(per_token, 6, axis=1)
    attn_in = low(layer_norm(embedded) * (1.0 + scale_a) + shift_a)
    triple = product(attn_in, heads_weight)
    queries = low_back(low(triple[:, :D] + query_bias))
    keys = low_back(low(triple[:, D:2 * D]))
    values = low_back(low(triple[:, 2 * D:] + value_bias))
    attended = low(low_back(attend(queries, keys, values, seg_flat)))
    branch_a = low_back(product(attended, merge_weight) + merge_bias)
    resid_a = embedded + gate_a * branch_a
    mlp_in = low(layer_norm(resid_a) * (1.0 + scale_b) + shift_b)
    upper = low_back(product(mlp_in, up_weight) + up_bias)
    gelu_low = low(jax.nn.gelu(upper, approximate=True))
    branch_b = low_back(product(gelu_low, down_weight) + down_bias)
    resid_b = resid_a + gate_b * branch_b
    pixels = low_back(product(low(resid_b), final_weight) + final_bias) * live_mask[:, None]
    canvas_out = pixels.reshape(height, breadth, CHANNELS, 2, 2).transpose(2, 0, 3, 1, 4).reshape(CHANNELS, 2 * height, 2 * breadth)
    return jnp.roll(canvas_out, (-1, -1), axis=(1, 2))

def reference(latent, context, segment, patch_weight, patch_bias, adaln_weight, adaln_bias, heads_weight, query_bias, value_bias, merge_weight, merge_bias, up_weight, up_bias, down_weight, down_bias, final_weight, final_bias, cotangent):
    params = tuple((item.astype(jnp.float32) for item in (patch_weight, patch_bias, adaln_weight, adaln_bias, heads_weight, query_bias, value_bias, merge_weight, merge_bias, up_weight, up_bias, down_weight, down_bias, final_weight, final_bias)))
    latent_f = latent.astype(jnp.float32)
    context_f = context.astype(jnp.float32).reshape(GROUPS, SLOTS, D)

    def forward(latent_all, context_all, weights):

        def group_step(inputs):
            return group_forward(weights, inputs[0], inputs[1], inputs[2])
        return lax.map(jax.checkpoint(group_step), (latent_all, context_all, segment))
    output, pullback = jax.vjp(forward, latent_f, context_f, params)
    grad_latent, grad_context, grads = pullback(cotangent.astype(jnp.float32))
    return (output, grad_latent, grad_context.reshape(GROUPS * SLOTS, D), grads[0], grads[1], grads[2], grads[3], grads[4], grads[5], grads[6], grads[7], grads[8], grads[9], grads[10], grads[11], grads[12], grads[13], grads[14])
```

```python
import math

import jax
import jax.numpy as jnp
from jax import lax
from jax.experimental import pallas as pl
from jax.experimental.pallas import tpu as pltpu
from jax.sharding import PartitionSpec as P

HEADS = 16
BLOCK = 32
EPSILON = 1e-06
MASKED = -1e30
F32 = jnp.float32
BF16 = jnp.bfloat16
VMEM_LIMIT = 60 * 1024 * 1024


def bf(tensor):
    return tensor.astype(BF16)


def dot(left, right, left_dim=1, right_dim=0):
    return lax.dot_general(
        left, right, (((left_dim,), (right_dim,)), ((), ())), preferred_element_type=F32
    )


def swap(array, axis, level):
    return lax.ppermute(array, axis, [(i, i ^ 1 << level) for i in range(lax.axis_size(axis))])


def bit_of(axis, level):
    return lax.axis_index(axis) >> level & 1


def half_of(array, which, dim):
    size = array.shape[dim] // 2
    return lax.dynamic_slice_in_dim(array, which * size, size, dim)


def pick(array, which, dim):
    return lax.dynamic_index_in_dim(array, which, dim, keepdims=False)


def full(shape):
    rank = len(shape)
    return pl.BlockSpec(shape, lambda *_: (0,) * rank)


def params(steps=1, **more):
    return pltpu.CompilerParams(
        dimension_semantics=("arbitrary",) * steps, vmem_limit_bytes=VMEM_LIMIT, **more
    )


def cost(flops, moved, trans=0):
    return pl.CostEstimate(flops=int(flops), bytes_accessed=int(moved), transcendentals=int(trans))


def normalize(tensor):
    center = tensor - jnp.mean(tensor, axis=-1, keepdims=True)
    rstd = lax.rsqrt(jnp.mean(center * center, axis=-1, keepdims=True) + EPSILON)
    return center * rstd, rstd


def norm_pull(normed, rstd, grad):
    return rstd * (
        grad
        - jnp.mean(grad, axis=-1, keepdims=True)
        - normed * jnp.mean(grad * normed, axis=-1, keepdims=True)
    )


def column_sum(tensor):
    return jnp.sum(tensor, axis=0, keepdims=True)


def modulation_rows(row, live, weight, bias, start, count, tile):
    depth = weight.shape[0]
    first = start // tile

    def kernel(live_ref, row_ref, weight_ref, bias_ref, out_ref):
        out = dot(row_ref[...], weight_ref[...]) + bias_ref[...].astype(F32)
        out_ref[...] = out * live_ref[0]

    return pl.pallas_call(
        kernel,
        grid=(count // tile,),
        in_specs=[
            pl.BlockSpec(memory_space=pltpu.SMEM),
            full((16, depth)),
            pl.BlockSpec((depth, tile), lambda i: (0, i + first)),
            pl.BlockSpec((1, tile), lambda i: (0, i + first)),
        ],
        out_specs=pl.BlockSpec((16, tile), lambda i: (0, i)),
        out_shape=jax.ShapeDtypeStruct((16, count), F32),
        compiler_params=params(),
        cost_estimate=cost(2 * 16 * depth * count, 2 * depth * count),
        name="modulation",
    )(live, row, weight, bias)


def embed_project(patches, patch_weight, base, shift, scale, weight, bias, start, count, tile):
    tokens, width = base.shape
    first = start // tile

    def kernel(
        pat_ref, pw_ref, base_ref, shift_ref, scale_ref, weight_ref, bias_ref, emb_ref, in_ref, out_ref
    ):
        @pl.when(pl.program_id(0) == 0)
        def _():
            emb = dot(pat_ref[...], pw_ref[...]) + base_ref[...]
            emb_ref[...] = emb
            normed, _ = normalize(emb)
            in_ref[...] = bf(normed * (1.0 + scale_ref[0:1, :]) + shift_ref[0:1, :])

        out = dot(in_ref[...], weight_ref[...]) + bias_ref[...]
        out_ref[...] = bf(out.T)

    return pl.pallas_call(
        kernel,
        grid=(count // tile,),
        in_specs=[
            full(patches.shape),
            full(patch_weight.shape),
            full((tokens, width)),
            full(shift.shape),
            full(scale.shape),
            pl.BlockSpec((width, tile), lambda i: (0, i + first)),
            pl.BlockSpec((1, tile), lambda i: (0, i + first)),
        ],
        out_specs=[
            full((tokens, width)),
            full((tokens, width)),
            pl.BlockSpec((tile, tokens), lambda i: (i, 0)),
        ],
        out_shape=[
            jax.ShapeDtypeStruct((tokens, width), F32),
            jax.ShapeDtypeStruct((tokens, width), BF16),
            jax.ShapeDtypeStruct((count, tokens), BF16),
        ],
        compiler_params=params(),
        cost_estimate=cost(2 * tokens * width * count, 2 * width * count + 12 * tokens * width),
        name="embed_project",
    )(patches, patch_weight, base, shift, scale, weight, bias)


def project(entry, weight, bias, start, count, tile):
    tokens, width = entry.shape
    first = start // tile

    def kernel(in_ref, weight_ref, bias_ref, out_ref):
        out = dot(in_ref[...], weight_ref[...]) + bias_ref[...]
        out_ref[...] = bf(out.T)

    return pl.pallas_call(
        kernel,
        grid=(count // tile,),
        in_specs=[
            full((tokens, width)),
            pl.BlockSpec((width, tile), lambda i: (0, i + first)),
            pl.BlockSpec((1, tile), lambda i: (0, i + first)),
        ],
        out_specs=pl.BlockSpec((tile, tokens), lambda i: (i, 0)),
        out_shape=jax.ShapeDtypeStruct((count, tokens), BF16),
        compiler_params=params(),
        cost_estimate=cost(2 * tokens * width * count, 2 * width * count + 4 * tokens * width),
        name="project",
    )(entry, weight, bias)


def attention_specs(group, head, tokens, tiles):
    steps = HEADS // group
    block = (group, head, tokens)
    specs = [pl.BlockSpec(block, lambda i: (i, 0, 0))]
    specs += [pl.BlockSpec(block, lambda i: (i, 0, 0))] * tiles
    specs += [pl.BlockSpec(block, lambda i: (i + steps, 0, 0))] * tiles
    return specs


def attention_forward(tile_bias, queries, pairs, scale, group):
    tiles = len(pairs)
    head, tokens = queries.shape[1:]
    factor = scale * math.log2(math.e)

    def kernel(bias_ref, q_ref, *refs):
        k_refs, v_refs = refs[:tiles], refs[tiles : 2 * tiles]
        out_ref, lse_ref = refs[2 * tiles :]
        lane = lax.broadcasted_iota(jnp.int32, lse_ref.shape, 1)
        step = pl.program_id(0)
        for h in range(group):
            keys = jnp.concatenate([ref[h] for ref in k_refs], axis=1)
            raw = dot(q_ref[h], keys, 0, 0)
            scores = [
                raw[:, j * tokens : (j + 1) * tokens] * factor + bias_ref[j] for j in range(tiles)
            ]
            top = scores[0]
            for part in scores[1:]:
                top = jnp.maximum(top, part)
            top = jnp.max(top, axis=1, keepdims=True)
            expo = [jnp.exp2(part - top) for part in scores]
            total = expo[0]
            for part in expo[1:]:
                total = total + part
            total = jnp.sum(total, axis=1, keepdims=True)
            inverse = 1.0 / total
            probs = jnp.concatenate([bf(part * inverse) for part in expo], axis=1)
            values = jnp.concatenate([ref[h] for ref in v_refs], axis=1)
            out_ref[h] = bf(dot(values, probs, 1, 1))
            lse_ref[...] = jnp.where(lane == step * group + h, top + jnp.log2(total), lse_ref[...])

    count = tiles * tokens
    return pl.pallas_call(
        kernel,
        grid=(HEADS // group,),
        in_specs=[pl.BlockSpec(memory_space=pltpu.SMEM)]
        + attention_specs(group, head, tokens, tiles),
        out_specs=[pl.BlockSpec((group, head, tokens), lambda i: (i, 0, 0)), full((tokens, 128))],
        out_shape=[
            jax.ShapeDtypeStruct((HEADS, head, tokens), BF16),
            jax.ShapeDtypeStruct((tokens, 128), F32),
        ],
        compiler_params=params(),
        cost_estimate=cost(
            4 * 256 * HEADS * tokens * count, 4 * HEADS * head * count, HEADS * tokens * count
        ),
        name="attention_forward",
    )(tile_bias, queries, *pairs, *pairs)


def attention_backward(tile_bias, queries, pairs, grads, lse, scale, group):
    tiles = len(pairs)
    head, tokens = queries.shape[1:]
    factor = scale * math.log2(math.e)

    def kernel(bias_ref, q_ref, *refs):
        k_refs, v_refs = refs[:tiles], refs[tiles : 2 * tiles]
        g_ref, lse_ref = refs[2 * tiles : 2 * tiles + 2]
        dq_ref = refs[2 * tiles + 2]
        dk_refs = refs[2 * tiles + 3 : 3 * tiles + 3]
        dv_refs = refs[3 * tiles + 3 :]
        lane = lax.broadcasted_iota(jnp.int32, lse_ref.shape, 1)
        step = pl.program_id(0)
        for h in range(group):
            mine = lane == step * group + h
            logsum = jnp.sum(jnp.where(mine, lse_ref[...], 0.0), axis=1, keepdims=True)
            keys = jnp.concatenate([ref[h] for ref in k_refs], axis=1)
            values = jnp.concatenate([ref[h] for ref in v_refs], axis=1)
            raw = dot(q_ref[h], keys, 0, 0)
            pull = dot(g_ref[h], values, 0, 0)
            probs = []
            delta = None
            for j in range(tiles):
                cut = slice(j * tokens, (j + 1) * tokens)
                prob = jnp.exp2(raw[:, cut] * factor + (bias_ref[j] - logsum))
                part = prob * pull[:, cut]
                delta = part if delta is None else delta + part
                probs.append(prob)
            delta = jnp.sum(delta, axis=1, keepdims=True)
            slopes = jnp.concatenate(
                [
                    bf(prob * (pull[:, j * tokens : (j + 1) * tokens] - delta))
                    for j, prob in enumerate(probs)
                ],
                axis=1,
            )
            probs = jnp.concatenate([bf(prob) for prob in probs], axis=1)
            dq_ref[h] = bf(dot(keys, slopes, 1, 1) * scale)
            grad_keys = dot(q_ref[h], slopes) * scale
            grad_values = dot(g_ref[h], probs)
            for j in range(tiles):
                cut = slice(j * tokens, (j + 1) * tokens)
                dk_refs[j][h] = bf(grad_keys[:, cut])
                dv_refs[j][h] = bf(grad_values[:, cut])

    block = pl.BlockSpec((group, head, tokens), lambda i: (i, 0, 0))
    shape = jax.ShapeDtypeStruct((HEADS, head, tokens), BF16)
    count = tiles * tokens
    return pl.pallas_call(
        kernel,
        grid=(HEADS // group,),
        in_specs=[pl.BlockSpec(memory_space=pltpu.SMEM)]
        + attention_specs(group, head, tokens, tiles)
        + [block, full((tokens, 128))],
        out_specs=[block] * (1 + 2 * tiles),
        out_shape=[shape] * (1 + 2 * tiles),
        compiler_params=params(),
        cost_estimate=cost(
            10 * 256 * HEADS * tokens * count, 8 * HEADS * head * count, HEADS * tokens * count
        ),
        name="attention_backward",
    )(tile_bias, queries, *pairs, *pairs, grads, lse)


GELU_A = math.sqrt(2.0 / math.pi)
GELU_B = 0.044715


def feed_forward(
    attended, merge_weight, merge_bias, embedded, rows, up_weight, up_bias, down_weight, cot,
    final_weight, tile
):
    tokens, width = embedded.shape
    hidden = up_weight.shape[1]

    def kernel(
        att_ref, mw_ref, mb_ref, emb_ref, rows_ref, up_ref, ub_ref, down_ref, cot_ref, fw_ref,
        resid_ref, branch_ref, in_ref, gbb_ref, gel_ref, gup_ref, ubg_ref, bb_ref, gin_ref
    ):
        @pl.when(pl.program_id(0) == 0)
        def _():
            branch = dot(att_ref[...], mw_ref[...], 0, 0) + mb_ref[...].astype(F32)
            branch_ref[...] = branch
            resid = emb_ref[...] + rows_ref[0:1, :] * branch
            resid_ref[...] = resid
            normed, _ = normalize(resid)
            in_ref[...] = bf(normed * (1.0 + rows_ref[2:3, :]) + rows_ref[1:2, :])
            grad_resid = dot(cot_ref[...], fw_ref[...], 1, 1)
            gbb_ref[...] = bf(grad_resid * rows_ref[3:4, :])
            bb_ref[...] = jnp.zeros_like(bb_ref)
            gin_ref[...] = jnp.zeros_like(gin_ref)

        upper = dot(in_ref[...], up_ref[...]) + ub_ref[...].astype(F32)
        square = upper * upper
        tanh = jnp.tanh(GELU_A * upper * (1.0 + GELU_B * square))
        half = 0.5 + 0.5 * tanh
        gelu = bf(upper * half)
        slope = half + 0.5 * upper * (1.0 - tanh * tanh) * (GELU_A * (1.0 + 3.0 * GELU_B * square))
        grad = dot(gbb_ref[...], down_ref[...], 1, 1)
        grad_upper = bf(slope * grad)
        bb_ref[...] += dot(gelu, down_ref[...])
        gin_ref[...] += dot(grad_upper, up_ref[...], 1, 1)
        ubg_ref[...] = column_sum(grad_upper.astype(F32))
        gel_ref[...] = gelu.T
        gup_ref[...] = grad_upper.T

    matrix = full((tokens, width))
    turned = pl.BlockSpec((tile, tokens), lambda i: (i, 0))
    return pl.pallas_call(
        kernel,
        grid=(hidden // tile,),
        in_specs=[
            full(attended.shape),
            full(merge_weight.shape),
            full((1, width)),
            matrix,
            full(rows.shape),
            pl.BlockSpec((width, tile), lambda i: (0, i)),
            pl.BlockSpec((1, tile), lambda i: (0, i)),
            pl.BlockSpec((tile, width), lambda i: (i, 0)),
            full(cot.shape),
            full(final_weight.shape),
        ],
        out_specs=[matrix, matrix, matrix, matrix, turned, turned,
                   pl.BlockSpec((1, tile), lambda i: (0, i)), matrix, matrix],
        out_shape=[
            jax.ShapeDtypeStruct((tokens, width), F32),
            jax.ShapeDtypeStruct((tokens, width), F32),
            jax.ShapeDtypeStruct((tokens, width), BF16),
            jax.ShapeDtypeStruct((tokens, width), BF16),
            jax.ShapeDtypeStruct((hidden, tokens), BF16),
            jax.ShapeDtypeStruct((hidden, tokens), BF16),
            jax.ShapeDtypeStruct((1, hidden), F32),
            jax.ShapeDtypeStruct((tokens, width), F32),
            jax.ShapeDtypeStruct((tokens, width), F32),
        ],
        compiler_params=params(),
        cost_estimate=cost(
            8 * tokens * width * hidden + 2 * tokens * width * width,
            4 * width * hidden + 2 * width * width + 24 * tokens * width,
            tokens * hidden,
        ),
        name="feed_forward",
    )(attended, merge_weight, merge_bias, embedded, rows, up_weight, up_bias, down_weight, cot,
      final_weight)


def feed_forward_end(
    resid, branch_a, gbb, branch_sum, grad_in, rows, down_bias, cot, final_weight, final_bias, live,
    merge_weight
):
    tokens, width = resid.shape
    pixels_count = cot.shape[1]

    def kernel(
        live_ref, resid_ref, branch_ref, gbb_ref, bb_ref, gin_ref, rows_ref, db_ref, cot_ref, fw_ref,
        fb_ref, mw_ref, gatt_ref, gba_ref, gres_ref, pix_ref, fwg_ref, sums_ref
    ):
        gate_a, scale_b, gate_b = rows_ref[0:1, :], rows_ref[2:3, :], rows_ref[3:4, :]
        cot_value = cot_ref[...]
        grad_resid = dot(cot_value, fw_ref[...], 1, 1)
        normed, rstd = normalize(resid_ref[...])
        grad_in_value = gin_ref[...]
        grad_resid_a = grad_resid + norm_pull(normed, rstd, grad_in_value * (1.0 + scale_b))
        gres_ref[...] = grad_resid_a
        grad_branch_a = bf(gate_a * grad_resid_a)
        gba_ref[...] = grad_branch_a
        gatt_ref[...] = bf(dot(mw_ref[...], grad_branch_a, 1, 1))
        branch_b = bb_ref[...] + db_ref[...].astype(F32)
        resid_low = bf(resid_ref[...] + gate_b * branch_b)
        pix_ref[...] = (dot(resid_low, fw_ref[...]) + fb_ref[...].astype(F32)) * live_ref[0]
        fwg_ref[...] = dot(cot_value, resid_low, 0, 0)
        sums_ref[0:1, :] = column_sum(grad_resid_a * branch_ref[...])
        sums_ref[1:2, :] = column_sum(grad_in_value)
        sums_ref[2:3, :] = column_sum(grad_in_value * normed)
        sums_ref[3:4, :] = column_sum(grad_resid * branch_b)
        sums_ref[4:5, :] = column_sum(gbb_ref[...].astype(F32))
        sums_ref[5:6, :] = column_sum(grad_branch_a.astype(F32))
        sums_ref[6:8, :] = jnp.zeros((2, width), F32)

    vmem = pl.BlockSpec(memory_space=pltpu.VMEM)
    return pl.pallas_call(
        kernel,
        in_specs=[pl.BlockSpec(memory_space=pltpu.SMEM)] + [vmem] * 11,
        out_specs=[vmem] * 6,
        out_shape=[
            jax.ShapeDtypeStruct((width, tokens), BF16),
            jax.ShapeDtypeStruct((tokens, width), BF16),
            jax.ShapeDtypeStruct((tokens, width), F32),
            jax.ShapeDtypeStruct((tokens, pixels_count), F32),
            jax.ShapeDtypeStruct((pixels_count, width), F32),
            jax.ShapeDtypeStruct((8, width), F32),
        ],
        compiler_params=pltpu.CompilerParams(vmem_limit_bytes=VMEM_LIMIT),
        cost_estimate=cost(2 * tokens * width * width, 2 * width * width + 26 * tokens * width),
        name="feed_forward_end",
    )(live, resid, branch_a, gbb, branch_sum, grad_in, rows, down_bias, cot, final_weight, final_bias,
      merge_weight)


def embed_backward(grads, weight, embedded, rows, grad_resid, patches, patch_weight, tile):
    tokens, width = embedded.shape
    count = weight.shape[1]
    steps = count // tile
    features = patches.shape[1]

    def kernel(
        g_ref, w_ref, emb_ref, rows_ref, gres_ref, pat_ref, pw_ref,
        bias_ref, lat_ref, pwg_ref, sums_ref, acc_ref
    ):
        step = pl.program_id(0)

        @pl.when(step == 0)
        def _():
            acc_ref[...] = jnp.zeros_like(acc_ref)

        acc_ref[...] += dot(g_ref[...], w_ref[...], 0, 1)
        bias_ref[...] = dot(jnp.ones((8, tokens), BF16), g_ref[...], 1, 1)

        @pl.when(step == steps - 1)
        def _():
            grad_in = acc_ref[...]
            normed, rstd = normalize(emb_ref[...])
            grad = gres_ref[...] + norm_pull(normed, rstd, grad_in * (1.0 + rows_ref[1:2, :]))
            grad_low = bf(grad)
            lat_ref[...] = dot(grad_low, pw_ref[...], 1, 1)
            pwg_ref[...] = dot(pat_ref[...], grad_low, 0, 0)
            sums_ref[0:1, :] = column_sum(grad_in)
            sums_ref[1:2, :] = column_sum(grad_in * normed)
            sums_ref[2:3, :] = column_sum(grad)
            sums_ref[3:8, :] = jnp.zeros((5, width), F32)

    matrix = full((tokens, width))
    return pl.pallas_call(
        kernel,
        grid=(steps,),
        in_specs=[
            pl.BlockSpec((tile, tokens), lambda i: (i, 0)),
            pl.BlockSpec((width, tile), lambda i: (0, i)),
            matrix,
            full(rows.shape),
            matrix,
            full(patches.shape),
            full(patch_weight.shape),
        ],
        out_specs=[
            pl.BlockSpec((8, tile), lambda i: (0, i)),
            full((tokens, features)),
            full((features, width)),
            full((8, width)),
        ],
        out_shape=[
            jax.ShapeDtypeStruct((8, count), F32),
            jax.ShapeDtypeStruct((tokens, features), F32),
            jax.ShapeDtypeStruct((features, width), F32),
            jax.ShapeDtypeStruct((8, width), F32),
        ],
        scratch_shapes=[pltpu.VMEM((tokens, width), F32)],
        compiler_params=params(),
        cost_estimate=cost(2 * tokens * width * count, 2 * width * count + 12 * tokens * width),
        name="embed_backward",
    )(grads, weight, embedded, rows, grad_resid, patches, patch_weight)


def halve(array, axis, level, dim):
    mine = bit_of(axis, level)
    got = swap(bf(half_of(array, 1 - mine, dim)), axis, level)
    return half_of(array, mine, dim).astype(F32) + got.astype(F32)


def rest_of_img(array):
    for level in reversed(range(lax.axis_size("img").bit_length() - 2)):
        array = halve(array, "img", level, 1)
    return array


def sum_by_columns(entry, grads_t):
    rows = entry.shape[1]
    top = lax.axis_size("img").bit_length() - 2
    mine = bit_of("img", top)
    entry_x = swap(entry, "img", top)
    grads_x = swap(half_of(grads_t, 1 - mine, 0), "img", top)
    entry = jnp.concatenate([entry, entry_x], axis=0)
    grads = jnp.concatenate([half_of(grads_t, mine, 0), grads_x], axis=1)
    core = bit_of("col", 0)
    entry_c = swap(entry, "col", 0)
    grads_c = swap(half_of(grads, 1 - core, 0), "col", 0)
    entry = jnp.concatenate([entry, entry_c], axis=0)
    grads = jnp.concatenate([half_of(grads, core, 0), grads_c], axis=1)
    share = bf(dot(entry, grads, 0, 1))
    columns = share.shape[1]
    share = share.reshape(4, 2, rows // 8, columns)
    share = bf(halve(share, "col", 1, 1)[:, 0]).reshape(2, 2, rows // 8, columns)
    share = bf(halve(share, "row", 0, 1)[:, 0])
    share = halve(share, "row", 1, 0)[0].reshape(2, rows // 16, columns)
    other = swap(bf(pick(share, 1 - core, 0)), "col", 0)
    own = bf(pick(share, core, 0))
    joined = jnp.where(
        core == 1, jnp.concatenate([other, own], axis=1), jnp.concatenate([own, other], axis=1)
    )
    return rest_of_img(joined.astype(F32))


def sum_by_rows(entry_t, grads):
    rows, tokens = entry_t.shape
    entry = entry_t.reshape(4, 2, 2, rows // 16, tokens)
    for level in (1, 0):
        mine = bit_of("col", level)
        dim = 2 - level
        grads_p = swap(grads, "col", level)
        entry_p = swap(pick(entry, 1 - mine, 1), "col", level)
        entry = jnp.concatenate([pick(entry, mine, 1), entry_p], axis=-1)
        grads = jnp.concatenate([grads, grads_p], axis=0)
    share = bf(dot(entry.reshape(rows // 4, entry.shape[-1]), grads))
    top = lax.axis_size("img").bit_length() - 2
    share = bf(halve(share, "img", top, 1))
    share = share.reshape(2, 2, rows // 16, share.shape[1])
    share = bf(halve(share, "row", 0, 1)[:, 0])
    share = halve(share, "row", 1, 0)[0]
    return rest_of_img(share)


def sum_all(array):
    for axis in ("col", "row", "img"):
        for level in range(lax.axis_size(axis).bit_length() - 1):
            array = array + swap(array, axis, level)
    return array


def gather_all(array, axis):
    for level in range(lax.axis_size(axis).bit_length() - 1):
        high = bit_of(axis, level) == 1
        other = swap(array, axis, level)
        array = jnp.where(
            high, jnp.concatenate([other, array], axis=0), jnp.concatenate([array, other], axis=0)
        )
    return array


def shifted(array, axes, by):
    sizes = [lax.axis_size(axis) for axis in axes]
    pairs = []
    total = math.prod(sizes)
    for index in range(total):
        rest, target, scale = index, 0, 1
        for size, step in reversed(list(zip(sizes, by))):
            target += (rest % size + step) % size * scale
            rest //= size
            scale *= size
        pairs.append((index, target))
    return lax.ppermute(array, axes, pairs)


def roll_in(tile):
    above = shifted(tile[:, -1:, :-1], ("row",), (1,))
    left = shifted(tile[:, :-1, -1:], ("col",), (1,))
    corner = shifted(tile[:, -1:, -1:], ("row", "col"), (1, 1))
    first = jnp.concatenate([corner, above], axis=2)
    rest = jnp.concatenate([left, tile[:, :-1, :-1]], axis=2)
    return jnp.concatenate([first, rest], axis=1)


def roll_out(tile):
    below = shifted(tile[:, :1, 1:], ("row",), (-1,))
    right = shifted(tile[:, 1:, :1], ("col",), (-1,))
    corner = shifted(tile[:, :1, :1], ("row", "col"), (-1, -1))
    last = jnp.concatenate([below, corner], axis=2)
    rest = jnp.concatenate([tile[:, 1:, 1:], right], axis=2)
    return jnp.concatenate([rest, last], axis=1)


def to_tokens(tile_data):
    channels, height, breadth = tile_data.shape
    return (
        tile_data.reshape(channels, height // 2, 2, breadth // 2, 2)
        .transpose(1, 3, 0, 2, 4)
        .reshape(height * breadth // 4, channels * 4)
    )


def to_tile(tokens, channels, height, breadth):
    return (
        tokens.reshape(height // 2, breadth // 2, channels, 2, 2)
        .transpose(2, 0, 3, 1, 4)
        .reshape(channels, height, breadth)
    )


def wave_table(index, quarter):
    frequency = 1.0 / 10000.0 ** (jnp.arange(quarter, dtype=F32) / quarter)
    angle = index.astype(F32)[:, None] * frequency[None, :]
    return jnp.concatenate([jnp.sin(angle), jnp.cos(angle)], axis=1)


def local(
    latent, context, segment, patch_weight, patch_bias, adaln_weight, adaln_bias, heads_weight,
    query_bias, value_bias, merge_weight, merge_bias, up_weight, up_bias, down_weight, down_bias,
    final_weight, final_bias, cotangent
):
    rows_count, cols_count = lax.axis_size("row"), lax.axis_size("col")
    row_index, col_index = lax.axis_index("row"), lax.axis_index("col")
    channels, height, breadth = latent.shape[1:]
    tile_rows, tile_cols = height // 2, breadth // 2
    assert tile_rows == BLOCK // 2 and tile_cols == BLOCK // 2
    assert rows_count == 4 and cols_count == 4
    tokens = tile_rows * tile_cols
    width = patch_weight.shape[1]
    head = width // HEADS
    scale = 1.0 / math.sqrt(head)
    slots = context.shape[0]

    ids = segment[0, ::tile_rows, ::tile_cols]
    slot = ids[row_index, col_index]
    partners = [
        ids[row_index ^ dz, col_index ^ dc] for dz, dc in ((0, 0), (0, 1), (1, 0), (1, 1))
    ]
    tile_bias = jnp.where(jnp.stack(partners) == slot, 0.0, MASKED).astype(F32)
    live = (slot >= 0).astype(F32)[None]
    is_large = slot % 5 == 4

    context_f = context.astype(F32)
    silu_out, silu_pull = jax.vjp(jax.nn.silu, context_f)
    context_low = bf(silu_out)
    row = lax.dynamic_slice_in_dim(context_low, jnp.maximum(slot, 0), 1, 0)
    row = jnp.broadcast_to(row, (16, width))
    adaln_bias2 = adaln_bias[None]
    mod_a = modulation_rows(row, live, adaln_weight, adaln_bias2, 0, 2 * width, 768)

    both = jnp.concatenate([latent[0], cotangent[0]], axis=0)
    both = roll_in(both)
    patches = to_tokens(both[:channels])
    cot = bf(to_tokens(both[channels:]).astype(F32) * live)
    grid_r = row_index * tile_rows + jnp.arange(tile_rows, dtype=jnp.int32)
    grid_c = col_index * tile_cols + jnp.arange(tile_cols, dtype=jnp.int32)
    wave_r = wave_table(jnp.where(is_large, grid_r % BLOCK, grid_r % (BLOCK // 2)), width // 4)
    wave_c = wave_table(jnp.where(is_large, grid_c % BLOCK, grid_c % (BLOCK // 2)), width // 4)
    half = width // 2
    base = jnp.concatenate(
        [
            jnp.broadcast_to(wave_r[:, None, :], (tile_rows, tile_cols, half)),
            jnp.broadcast_to(wave_c[None, :, :], (tile_rows, tile_cols, half)),
        ],
        axis=2,
    ).reshape(tokens, width) + patch_bias.astype(F32)

    bias3 = jnp.concatenate(
        [query_bias.astype(F32), jnp.zeros((width,), F32), value_bias.astype(F32)]
    )[None]
    shift_a, scale_a = mod_a[:, :width], mod_a[:, width:]
    embedded, attn_in, pair_own = embed_project(
        patches, patch_weight, base, shift_a, scale_a, heads_weight, bias3, width, 2 * width, 384
    )
    pair_z = swap(pair_own, "row", 0)
    pair_c = swap(pair_own, "col", 0)
    queries = project(attn_in, heads_weight, bias3, 0, width, 384)
    mod_b = modulation_rows(row, live, adaln_weight, adaln_bias2, 2 * width, 4 * width, 768)
    rows_b = jnp.concatenate([mod_b[0:1].reshape(4, width), jnp.zeros((4, width), F32)], axis=0)
    pair_zc = swap(pair_z, "col", 0)
    by_head = lambda array: array.reshape(-1, head, tokens)
    queries_h = by_head(queries)
    pairs = [by_head(pair) for pair in (pair_own, pair_c, pair_z, pair_zc)]
    attended, lse = attention_forward(tile_bias, queries_h, pairs, scale, 2)
    attended_t = attended.reshape(width, tokens)

    resid_a, branch_a, mlp_in, grad_branch_b, gelu_t, grad_upper_t, up_bias_grad, branch_sum, grad_in = (
        feed_forward(
            attended_t, merge_weight, merge_bias[None], embedded, rows_b, up_weight, up_bias[None],
            down_weight, cot, final_weight, 512,
        )
    )
    grad_att, grad_branch_a, grad_resid_a, pixels, final_grad_t, sums_b = feed_forward_end(
        resid_a, branch_a, grad_branch_b, branch_sum, grad_in, rows_b, down_bias[None], cot,
        final_weight, final_bias[None], live, merge_weight,
    )
    up_weight_grad = sum_by_columns(mlp_in, grad_upper_t)
    down_weight_grad = sum_by_rows(gelu_t, grad_branch_b)

    outs = attention_backward(
        tile_bias, queries_h, pairs, by_head(grad_att), lse, scale, 2
    )
    grad_q, grad_k, grad_v = outs[0], outs[1:5], outs[5:9]
    shares = [jnp.concatenate([grad_k[j], grad_v[j]], axis=0) for j in range(4)]
    got_zc = swap(shares[3], "col", 0)
    got_c = swap(shares[1], "col", 0)
    for_z = bf(shares[2].astype(F32) + got_zc.astype(F32))
    got_z = swap(for_z, "row", 0)
    pair_grad = bf(shares[0].astype(F32) + got_c.astype(F32) + got_z.astype(F32))
    triple = jnp.concatenate([grad_q, pair_grad], axis=0).reshape(3 * width, tokens)
    merge_weight_grad = sum_by_rows(attended_t, grad_branch_a)
    heads_weight_grad = sum_by_columns(attn_in, triple)

    rows_a = jnp.concatenate([shift_a[0:1], scale_a[0:1], jnp.zeros((6, width), F32)], axis=0)
    bias_sums, grad_patches, patch_weight_grad, sums_a = embed_backward(
        triple, heads_weight, embedded, rows_a, grad_resid_a, patches, patch_weight, 384
    )

    tiles_out = jnp.concatenate(
        [
            to_tile(pixels, channels, height, breadth),
            to_tile(grad_patches, channels, height, breadth),
        ],
        axis=0,
    )
    rolled = roll_out(tiles_out)

    final_bias_grad = jnp.sum(cot.astype(F32), axis=0)
    hidden = up_weight.shape[1]
    early = jnp.concatenate(
        [
            final_grad_t,
            up_bias_grad.reshape(hidden // width, width),
            sums_b[4:6],
            jnp.pad(final_bias_grad[None], ((0, 0), (0, width - final_bias_grad.shape[0]))),
        ],
        axis=0,
    )
    early = sum_all(early)
    late = jnp.concatenate(
        [patch_weight_grad, sums_a[2:3], bias_sums[0:1].reshape(3, width)], axis=0
    )
    late = sum_all(late)
    features = patches.shape[1]
    extra = features + hidden // width

    mod_early = jnp.concatenate([sums_b[0:1], sums_b[1:4]], axis=0).reshape(1, 4 * width)
    gathered_b = gather_all(gather_all(bf(mod_early), "col"), "row")
    gathered_a = gather_all(gather_all(bf(sums_a[0:2].reshape(1, 2 * width)), "col"), "row")
    gathered = jnp.concatenate([gathered_a, gathered_b], axis=1)
    flat_ids = ids.reshape(-1)
    select = (jnp.arange(slots, dtype=jnp.int32)[:, None] == flat_ids[None, :]).astype(BF16)
    grad_mod = bf(dot(select, gathered))
    (context_gradient,) = silu_pull(dot(grad_mod, adaln_weight, 1, 1))
    all_mod = gather_all(grad_mod, "img")
    all_context = gather_all(context_low, "img")
    adaln_bias_grad = jnp.sum(all_mod.astype(F32), axis=0)
    share = width // (rows_count * cols_count)
    flat = row_index * cols_count + col_index
    images = lax.axis_size("img")
    part = 6 * width // images
    context_rows = lax.dynamic_slice_in_dim(all_context, flat * share, share, 1)
    mod_cols = lax.dynamic_slice_in_dim(all_mod, lax.axis_index("img") * part, part, 1)
    adaln_weight_grad = dot(context_rows, mod_cols, 0, 0)

    return (
        rolled[:channels][None],
        rolled[channels:][None],
        context_gradient,
        late[:features],
        late[features],
        adaln_weight_grad,
        adaln_bias_grad,
        heads_weight_grad,
        late[features + 1],
        late[features + 3],
        merge_weight_grad,
        early[extra + 1],
        up_weight_grad,
        early[features:extra].reshape(hidden),
        down_weight_grad,
        early[extra],
        early[:features].T,
        early[extra + 2, :final_bias_grad.shape[0]],
    )


def solution(mesh):
    tile = P("img", None, "row", "col")
    share = P(("row", "col"), "img")
    none = P()
    in_specs = (tile, P("img", None), P("img", None, None)) + (none,) * 15 + (tile,)
    out_specs = (
        tile, tile, P("img", None), none, none, share, none, share, none, none, share, none, share,
        none, share, none, none, none
    )
    return jax.shard_map(local, mesh=mesh, in_specs=in_specs, out_specs=out_specs, check_vma=False)
```

```python
import math

import jax
import jax.numpy as jnp
from jax import lax
from jax.experimental import pallas as pl
from jax.experimental.pallas import tpu as pltpu
from jax.sharding import PartitionSpec as P

HEADS = 16
BLOCK = 32
EPSILON = 1e-06
MASKED = -1e30
F32 = jnp.float32
BF16 = jnp.bfloat16
VMEM_LIMIT = 60 * 1024 * 1024


def bf(tensor):
    return tensor.astype(BF16)


def dot(left, right, left_dim=1, right_dim=0):
    return lax.dot_general(
        left, right, (((left_dim,), (right_dim,)), ((), ())), preferred_element_type=F32
    )


def swap(array, axis, level):
    return lax.ppermute(array, axis, [(i, i ^ 1 << level) for i in range(lax.axis_size(axis))])


def bit_of(axis, level):
    return lax.axis_index(axis) >> level & 1


def half_of(array, which, dim):
    size = array.shape[dim] // 2
    return lax.dynamic_slice_in_dim(array, which * size, size, dim)


def pick(array, which, dim):
    return lax.dynamic_index_in_dim(array, which, dim, keepdims=False)


def full(shape):
    rank = len(shape)
    return pl.BlockSpec(shape, lambda *_: (0,) * rank)


def params(steps=1, **more):
    return pltpu.CompilerParams(
        dimension_semantics=("arbitrary",) * steps, vmem_limit_bytes=VMEM_LIMIT, **more
    )


def cost(flops, moved, trans=0):
    return pl.CostEstimate(flops=int(flops), bytes_accessed=int(moved), transcendentals=int(trans))


def normalize(tensor):
    center = tensor - jnp.mean(tensor, axis=-1, keepdims=True)
    rstd = lax.rsqrt(jnp.mean(center * center, axis=-1, keepdims=True) + EPSILON)
    return center * rstd, rstd


def norm_pull(normed, rstd, grad):
    return rstd * (
        grad
        - jnp.mean(grad, axis=-1, keepdims=True)
        - normed * jnp.mean(grad * normed, axis=-1, keepdims=True)
    )


def column_sum(tensor):
    return jnp.sum(tensor, axis=0, keepdims=True)


def modulation_rows(row, live, weight, bias, start, count, tile):
    depth = weight.shape[0]
    first = start // tile

    def kernel(live_ref, row_ref, weight_ref, bias_ref, out_ref):
        out = dot(row_ref[...], weight_ref[...]) + bias_ref[...].astype(F32)
        out_ref[...] = out * live_ref[0]

    return pl.pallas_call(
        kernel,
        grid=(count // tile,),
        in_specs=[
            pl.BlockSpec(memory_space=pltpu.SMEM),
            full((16, depth)),
            pl.BlockSpec((depth, tile), lambda i: (0, i + first)),
            pl.BlockSpec((1, tile), lambda i: (0, i + first)),
        ],
        out_specs=pl.BlockSpec((16, tile), lambda i: (0, i)),
        out_shape=jax.ShapeDtypeStruct((16, count), F32),
        compiler_params=params(),
        cost_estimate=cost(2 * 16 * depth * count, 2 * depth * count),
        name="modulation",
    )(live, row, weight, bias)


def embed_project(patches, patch_weight, base, shift, scale, weight, bias, start, count, tile):
    tokens, width = base.shape
    first = start // tile

    def kernel(
        pat_ref, pw_ref, base_ref, shift_ref, scale_ref, weight_ref, bias_ref, emb_ref, in_ref, turned_ref, out_ref
    ):
        @pl.when(pl.program_id(0) == 0)
        def _():
            emb = dot(pat_ref[...], pw_ref[...]) + base_ref[...]
            emb_ref[...] = emb
            normed, _ = normalize(emb)
            entry = bf(normed * (1.0 + scale_ref[0:1, :]) + shift_ref[0:1, :])
            in_ref[...] = entry
            turned_ref[...] = entry.T

        out = dot(in_ref[...], weight_ref[...]) + bias_ref[...]
        out_ref[...] = bf(out.T)

    return pl.pallas_call(
        kernel,
        grid=(count // tile,),
        in_specs=[
            full(patches.shape),
            full(patch_weight.shape),
            full((tokens, width)),
            full(shift.shape),
            full(scale.shape),
            pl.BlockSpec((width, tile), lambda i: (0, i + first)),
            pl.BlockSpec((1, tile), lambda i: (0, i + first)),
        ],
        out_specs=[
            full((tokens, width)),
            full((tokens, width)),
            full((width, tokens)),
            pl.BlockSpec((tile, tokens), lambda i: (i, 0)),
        ],
        out_shape=[
            jax.ShapeDtypeStruct((tokens, width), F32),
            jax.ShapeDtypeStruct((tokens, width), BF16),
            jax.ShapeDtypeStruct((width, tokens), BF16),
            jax.ShapeDtypeStruct((count, tokens), BF16),
        ],
        compiler_params=params(),
        cost_estimate=cost(2 * tokens * width * count, 2 * width * count + 12 * tokens * width),
        name="embed_project",
    )(patches, patch_weight, base, shift, scale, weight, bias)


def project(entry, weight, bias, start, count, tile):
    tokens, width = entry.shape
    first = start // tile

    def kernel(in_ref, weight_ref, bias_ref, out_ref):
        out = dot(in_ref[...], weight_ref[...]) + bias_ref[...]
        out_ref[...] = bf(out.T)

    return pl.pallas_call(
        kernel,
        grid=(count // tile,),
        in_specs=[
            full((tokens, width)),
            pl.BlockSpec((width, tile), lambda i: (0, i + first)),
            pl.BlockSpec((1, tile), lambda i: (0, i + first)),
        ],
        out_specs=pl.BlockSpec((tile, tokens), lambda i: (i, 0)),
        out_shape=jax.ShapeDtypeStruct((count, tokens), BF16),
        compiler_params=params(),
        cost_estimate=cost(2 * tokens * width * count, 2 * width * count + 4 * tokens * width),
        name="project",
    )(entry, weight, bias)


def attention_specs(group, head, tokens, tiles):
    steps = HEADS // group
    block = (group, head, tokens)
    specs = [pl.BlockSpec(block, lambda i: (i, 0, 0))]
    specs += [pl.BlockSpec(block, lambda i: (i, 0, 0))] * tiles
    specs += [pl.BlockSpec(block, lambda i: (i + steps, 0, 0))] * tiles
    return specs


def attention_forward(tile_bias, queries, pairs, scale, group):
    tiles = len(pairs)
    head, tokens = queries.shape[1:]
    factor = scale * math.log2(math.e)

    def kernel(bias_ref, q_ref, *refs):
        k_refs, v_refs = refs[:tiles], refs[tiles : 2 * tiles]
        out_ref, lse_ref = refs[2 * tiles :]
        lane = lax.broadcasted_iota(jnp.int32, lse_ref.shape, 1)
        step = pl.program_id(0)
        for h in range(group):
            keys = jnp.concatenate([ref[h] for ref in k_refs], axis=1)
            raw = dot(q_ref[h], keys, 0, 0)
            scores = [
                raw[:, j * tokens : (j + 1) * tokens] * factor + bias_ref[j] for j in range(tiles)
            ]
            top = scores[0]
            for part in scores[1:]:
                top = jnp.maximum(top, part)
            top = jnp.max(top, axis=1, keepdims=True)
            expo = [jnp.exp2(part - top) for part in scores]
            total = expo[0]
            for part in expo[1:]:
                total = total + part
            total = jnp.sum(total, axis=1, keepdims=True)
            inverse = 1.0 / total
            probs = jnp.concatenate([bf(part * inverse) for part in expo], axis=1)
            values = jnp.concatenate([ref[h] for ref in v_refs], axis=1)
            out_ref[h] = bf(dot(values, probs, 1, 1))
            lse_ref[...] = jnp.where(lane == step * group + h, top + jnp.log2(total), lse_ref[...])

    count = tiles * tokens
    return pl.pallas_call(
        kernel,
        grid=(HEADS // group,),
        in_specs=[pl.BlockSpec(memory_space=pltpu.SMEM)]
        + attention_specs(group, head, tokens, tiles),
        out_specs=[pl.BlockSpec((group, head, tokens), lambda i: (i, 0, 0)), full((tokens, 128))],
        out_shape=[
            jax.ShapeDtypeStruct((HEADS, head, tokens), BF16),
            jax.ShapeDtypeStruct((tokens, 128), F32),
        ],
        compiler_params=params(),
        cost_estimate=cost(
            4 * 256 * HEADS * tokens * count, 4 * HEADS * head * count, HEADS * tokens * count
        ),
        name="attention_forward",
    )(tile_bias, queries, *pairs, *pairs)


GELU_A = math.sqrt(2.0 / math.pi)
GELU_B = 0.044715
GROUP = 2


def middle(
    live, tile_bias, attended, merge_weight, merge_bias, embedded, rows, up_weight, up_bias, down_weight,
    down_bias, cot, final_weight, final_bias, queries, pairs, lse, scale
):
    tokens, width = embedded.shape
    hidden = up_weight.shape[1]
    features = cot.shape[1]
    tiles = len(pairs)
    head = width // HEADS
    parts = hidden // width
    assert parts == 4 and tiles == 4
    end = parts
    first_head = parts + 1
    groups = HEADS // GROUP
    last = first_head + groups
    factor = scale * math.log2(math.e)
    sub = width // 2
    att_sub = width // 8
    top = lax.axis_size("img").bit_length() - 2

    def kernel(
        live_ref, bias_ref, att_ref, mw_ref, mb_ref, emb_ref, rows_ref, up_ref, ub_ref, down_ref, db_ref,
        cot_ref, fw_ref, fb_ref, q_ref, *refs
    ):
        k_refs, v_refs, lse_ref = refs[:tiles], refs[tiles : 2 * tiles], refs[2 * tiles]
        (
            pix_ref, fwg_ref, sums_ref, ubg_ref, in_t_ref, gbb_t_ref, gel_ref, gup_ref, gba_t_ref, gres_ref,
            triple_ref, got_a, got_ay, got_b, got_by, got_m, got_my,
            in_ref, gbb_ref, resid_ref, branch_ref, bb_ref, gin_ref, gatt_ref,
            share_0, share_1, share_2, share_3, got_1, got_3, for_z, got_z,
            a_sent, a_came, b_sent, b_came, m_sent, m_came, c_sent, c_came, z_sent, z_came
        ) = refs[2 * tiles + 1 :]
        step = pl.program_id(0)
        x_me, y_me = lax.axis_index("img") >> top & 1, lax.axis_index("col") >> 1 & 1
        to_x = {"img": lax.axis_index("img") ^ 1 << top}
        to_y = {"col": lax.axis_index("col") ^ 2}
        to_c = {"col": lax.axis_index("col") ^ 1}
        to_z = {"row": lax.axis_index("row") ^ 1}

        def copy(source, target, sent, came, device):
            return pltpu.make_async_remote_copy(
                src_ref=source, dst_ref=target, send_sem=sent, recv_sem=came, device_id=device,
                device_id_type=pl.DeviceIdType.MESH,
            )

        def strip(ref, start, size):
            return ref.at[pl.ds(pl.multiple_of(start, math.gcd(size, sub)), size)]

        def send_entry():
            return copy(in_t_ref, got_a, a_sent.at[0], a_came.at[0], to_x)

        def send_upper(tile):
            slot = tile % 2
            return copy(
                strip(gup_ref, tile * width, width), strip(got_ay, slot * width, width),
                a_sent.at[1 + slot], a_came.at[1 + slot], to_x,
            )

        def send_branch():
            return copy(gbb_t_ref, got_by, b_sent.at[4], b_came.at[4], to_y)

        def send_gelu(tile):
            return copy(
                strip(gel_ref, tile * width + (1 - y_me) * sub, sub), strip(got_b, tile * sub, sub),
                b_sent.at[tile], b_came.at[tile], to_y,
            )

        def send_attended(tile):
            return copy(
                strip(att_ref, (2 * tile + 1 - y_me) * att_sub, att_sub),
                strip(got_m, tile * att_sub, att_sub), m_sent.at[tile], m_came.at[tile], to_y,
            )

        def send_merge():
            return copy(gba_t_ref, got_my, m_sent.at[4], m_came.at[4], to_y)

        def send_core(which, group):
            source, target = ((share_1, got_1), (share_3, got_3))[which]
            at = pl.ds(group * GROUP, GROUP)
            return copy(
                source.at[:, at], target.at[:, at], c_sent.at[which, group], c_came.at[which, group], to_c
            )

        def send_z(group):
            at = pl.ds(group * GROUP, GROUP)
            return copy(for_z.at[:, at], got_z.at[:, at], z_sent.at[group], z_came.at[group], to_z)

        def pass_on(group):
            at = pl.ds(group * GROUP, GROUP)
            send_core(1, group).wait_recv()
            for_z[:, at] = bf(share_2[:, at].astype(F32) + got_3[:, at].astype(F32))
            send_z(group).start()

        @pl.when(step == 0)
        def _():
            barrier = pltpu.get_barrier_semaphore()
            for device in (to_x, to_y, to_c, to_z):
                pl.semaphore_signal(
                    barrier, inc=1, device_id=device, device_id_type=pl.DeviceIdType.MESH
                )
            pl.semaphore_wait(barrier, 4)
            branch = dot(att_ref[...], mw_ref[...], 0, 0) + mb_ref[...].astype(F32)
            branch_ref[...] = branch
            resid = emb_ref[...] + rows_ref[0:1, :] * branch
            resid_ref[...] = resid
            normed, _ = normalize(resid)
            entry = bf(normed * (1.0 + rows_ref[2:3, :]) + rows_ref[1:2, :])
            in_ref[...] = entry
            in_t_ref[...] = entry.T
            send_entry().start()
            grad_resid = dot(cot_ref[...], fw_ref[...], 1, 1)
            gbb = bf(grad_resid * rows_ref[3:4, :])
            gbb_ref[...] = gbb
            gbb_t_ref[...] = gbb.T
            send_branch().start()
            sums_ref[5:6, :] = column_sum(gbb.astype(F32))
            bb_ref[...] = jnp.zeros_like(bb_ref)
            gin_ref[...] = jnp.zeros_like(gin_ref)

        @pl.when(step < end)
        def _():
            for cut in range(2):
                at = slice(cut * sub, (cut + 1) * sub)
                up_part, down_part = up_ref[:, at], down_ref[at, :]
                upper = dot(in_ref[...], up_part) + ub_ref[:, at].astype(F32)
                square = upper * upper
                tanh = jnp.tanh(GELU_A * upper * (1.0 + GELU_B * square))
                half = 0.5 + 0.5 * tanh
                gelu = bf(upper * half)
                slope = half + 0.5 * upper * (1.0 - tanh * tanh) * (
                    GELU_A * (1.0 + 3.0 * GELU_B * square)
                )
                grad = dot(gbb_ref[...], down_part, 1, 1)
                grad_upper = bf(slope * grad)
                bb_ref[...] += dot(gelu, down_part)
                gin_ref[...] += dot(grad_upper, up_part, 1, 1)
                ubg_ref[:, at] = column_sum(grad_upper.astype(F32))
                rows_at = pl.ds(pl.multiple_of(step * width + cut * sub, sub), sub)
                gel_ref[rows_at] = gelu.T
                gup_ref[rows_at] = grad_upper.T
            send_gelu(step).start()

            @pl.when(step // 2 != x_me)
            def _():
                send_upper(step).start()

        @pl.when(step == end)
        def _():
            gate_a, scale_b, gate_b = rows_ref[0:1, :], rows_ref[2:3, :], rows_ref[3:4, :]
            cot_value = cot_ref[...]
            grad_resid = dot(cot_value, fw_ref[...], 1, 1)
            normed, rstd = normalize(resid_ref[...])
            grad_in_value = gin_ref[...]
            grad_resid_a = grad_resid + norm_pull(normed, rstd, grad_in_value * (1.0 + scale_b))
            gres_ref[...] = grad_resid_a
            grad_branch_a = bf(gate_a * grad_resid_a)
            gba_t_ref[...] = grad_branch_a.T
            send_merge().start()
            for tile in range(4):
                send_attended(tile).start()
            grad_att = dot(mw_ref[...], grad_branch_a, 1, 1)
            for h in range(HEADS):
                gatt_ref[h] = bf(grad_att[h * head : (h + 1) * head])
            branch_b = bb_ref[...] + db_ref[...].astype(F32)
            resid_low = bf(resid_ref[...] + gate_b * branch_b)
            pix_ref[...] = (dot(resid_low, fw_ref[...]) + fb_ref[...].astype(F32)) * live_ref[0]
            fwg_ref[...] = dot(cot_value, resid_low, 0, 0)
            sums_ref[0:1, :] = column_sum(grad_resid_a * branch_ref[...])
            sums_ref[1:2, :] = column_sum(grad_in_value)
            sums_ref[2:3, :] = column_sum(grad_in_value * normed)
            sums_ref[3:4, :] = column_sum(grad_resid * branch_b)
            sums_ref[4:5, :] = column_sum(grad_branch_a.astype(F32))
            sums_ref[6:8, :] = jnp.zeros((2, width), F32)

        @pl.when((step >= first_head) & (step < last))
        def _():
            group = step - first_head
            lane = lax.broadcasted_iota(jnp.int32, lse_ref.shape, 1)
            for h in range(GROUP):
                index = group * GROUP + h
                logsum = jnp.sum(
                    jnp.where(lane == index, lse_ref[...], 0.0), axis=1, keepdims=True
                )
                grad = gatt_ref[index]
                keys = jnp.concatenate([ref[h] for ref in k_refs], axis=1)
                values = jnp.concatenate([ref[h] for ref in v_refs], axis=1)
                raw = dot(q_ref[h], keys, 0, 0)
                pull = dot(grad, values, 0, 0)
                probs = []
                delta = None
                for j in range(tiles):
                    cut = slice(j * tokens, (j + 1) * tokens)
                    prob = jnp.exp2(raw[:, cut] * factor + (bias_ref[j] - logsum))
                    part = prob * pull[:, cut]
                    delta = part if delta is None else delta + part
                    probs.append(prob)
                delta = jnp.sum(delta, axis=1, keepdims=True)
                slopes = jnp.concatenate(
                    [
                        bf(prob * (pull[:, j * tokens : (j + 1) * tokens] - delta))
                        for j, prob in enumerate(probs)
                    ],
                    axis=1,
                )
                probs = jnp.concatenate([bf(prob) for prob in probs], axis=1)
                triple_ref[0, index] = bf(dot(keys, slopes, 1, 1) * scale)
                grad_keys = dot(q_ref[h], slopes) * scale
                grad_values = dot(grad, probs)
                for j, share in enumerate((share_0, share_1, share_2, share_3)):
                    cut = slice(j * tokens, (j + 1) * tokens)
                    share[0, index] = bf(grad_keys[:, cut])
                    share[1, index] = bf(grad_values[:, cut])
            send_core(1, group).start()
            send_core(0, group).start()

            @pl.when(group > 0)
            def _():
                pass_on(group - 1)

        @pl.when(step == last)
        def _():
            pass_on(groups - 1)
            for group in range(groups):
                at = pl.ds(group * GROUP, GROUP)
                send_core(0, group).wait_recv()
                send_z(group).wait_recv()
                triple_ref[1:3, at] = bf(
                    share_0[:, at].astype(F32) + got_1[:, at].astype(F32) + got_z[:, at].astype(F32)
                )
                send_core(0, group).wait_send()
                send_core(1, group).wait_send()
                send_z(group).wait_send()
            send_entry().wait()
            for slot in range(2):
                send_upper((1 - x_me) * 2 + slot).wait()
            send_branch().wait()
            send_merge().wait()
            for tile in range(4):
                send_gelu(tile).wait()
                send_attended(tile).wait()

    matrix = full((tokens, width))
    turned = full((width, tokens))
    anywhere = pl.BlockSpec(memory_space=pl.ANY)
    smem = pl.BlockSpec(memory_space=pltpu.SMEM)
    at_part = lambda i: jnp.minimum(i, parts - 1)
    at_group = lambda i: jnp.clip(i - first_head, 0, groups - 1)
    block = (GROUP, head, tokens)
    own = pl.BlockSpec(block, lambda i: (at_group(i), 0, 0))
    other = pl.BlockSpec(block, lambda i: (at_group(i) + groups, 0, 0))
    share = pltpu.VMEM((2, HEADS, head, tokens), BF16)
    dma = pltpu.SemaphoreType.DMA
    return pl.pallas_call(
        kernel,
        grid=(last + 1,),
        in_specs=[
            smem, smem,
            full(attended.shape),
            full(merge_weight.shape),
            full((1, width)),
            matrix,
            full(rows.shape),
            pl.BlockSpec((width, width), lambda i: (0, at_part(i))),
            pl.BlockSpec((1, width), lambda i: (0, at_part(i))),
            pl.BlockSpec((width, width), lambda i: (at_part(i), 0)),
            full((1, width)),
            full(cot.shape),
            full(final_weight.shape),
            full((1, features)),
            own,
        ]
        + [own] * tiles
        + [other] * tiles
        + [full((tokens, 128))],
        out_specs=[
            full((tokens, features)),
            full((features, width)),
            full((8, width)),
            pl.BlockSpec((1, width), lambda i: (0, at_part(i))),
            turned,
            turned,
            full((hidden, tokens)),
            full((hidden, tokens)),
            turned,
            matrix,
            full((3, HEADS, head, tokens)),
            anywhere,
            anywhere,
            anywhere,
            anywhere,
            anywhere,
            anywhere,
        ],
        out_shape=[
            jax.ShapeDtypeStruct((tokens, features), F32),
            jax.ShapeDtypeStruct((features, width), F32),
            jax.ShapeDtypeStruct((8, width), F32),
            jax.ShapeDtypeStruct((1, hidden), F32),
            jax.ShapeDtypeStruct((width, tokens), BF16),
            jax.ShapeDtypeStruct((width, tokens), BF16),
            jax.ShapeDtypeStruct((hidden, tokens), BF16),
            jax.ShapeDtypeStruct((hidden, tokens), BF16),
            jax.ShapeDtypeStruct((width, tokens), BF16),
            jax.ShapeDtypeStruct((tokens, width), F32),
            jax.ShapeDtypeStruct((3, HEADS, head, tokens), BF16),
            jax.ShapeDtypeStruct((width, tokens), BF16),
            jax.ShapeDtypeStruct((2 * width, tokens), BF16),
            jax.ShapeDtypeStruct((2 * width, tokens), BF16),
            jax.ShapeDtypeStruct((width, tokens), BF16),
            jax.ShapeDtypeStruct((sub, tokens), BF16),
            jax.ShapeDtypeStruct((width, tokens), BF16),
        ],
        scratch_shapes=[
            pltpu.VMEM((tokens, width), BF16),
            pltpu.VMEM((tokens, width), BF16),
            pltpu.VMEM((tokens, width), F32),
            pltpu.VMEM((tokens, width), F32),
            pltpu.VMEM((tokens, width), F32),
            pltpu.VMEM((tokens, width), F32),
            pltpu.VMEM((HEADS, head, tokens), BF16),
        ]
        + [share] * 8
        + [
            dma((3,)), dma((3,)), dma((5,)), dma((5,)), dma((5,)), dma((5,)),
            dma((2, groups)), dma((2, groups)), dma((groups,)), dma((groups,)),
        ],
        compiler_params=params(collective_id=0, has_side_effects=True),
        cost_estimate=cost(
            8 * tokens * width * hidden + 10 * 256 * HEADS * tokens * tiles * tokens,
            4 * width * hidden + 4 * width * width + 24 * tokens * width,
            tokens * hidden + HEADS * tokens * tiles * tokens,
        ),
        name="middle",
    )(
        live, tile_bias, attended, merge_weight, merge_bias, embedded, rows, up_weight, up_bias, down_weight,
        down_bias, cot, final_weight, final_bias, queries, *pairs, *pairs, lse
    )


SUMS = 56
SLOT_ROWS = 32


def tail(
    features_in, got_up, got_up_y, got_down, got_down_y, got_att, got_merge, entry_heads, triple, heads_weight,
    adaln_weight, embedded, grad_resid, patches, patch_weight, rows_a, final_grad, up_sums, rows_sums,
    final_bias_grad, select, silu_slope, context_rows
):
    mlp_in, upper_t, gelu_t, branch_t, attended_h, merge_t = features_in
    width, tokens = mlp_in.shape
    hidden = upper_t.shape[0]
    half_hidden, half_heads = hidden // 2, 3 * width // 2
    quarter = half_heads // 2
    block = width // 8
    head = width // HEADS
    wide = hidden // 16
    half = width // 2
    images = lax.axis_size("img")
    top = images.bit_length() - 2
    pixels_count = patches.shape[1]
    all_tokens = 4 * tokens
    up_cuts = [(k * 384, 384) for k in range(width // 384)]
    down_cuts = [(k * 96, 96) for k in range(wide // 96)]
    padded = pl.cdiv(quarter, 128) * 128
    head_cuts = [(0, 384), (384, padded - 384)]

    def kernel(
        in_ref, gup_ref, gel_ref, gbb_ref, att_ref, gba_ref, gotu_x, gotu_y, gotd_x, gotd_y, gotm_x, gotm_y,
        xh_in, triple_ref, hw_ref, aw_ref, emb_ref, gres_ref, pat_ref, pw_ref, rows_ref, fwg_ref, ubg_ref,
        rsum_ref, fbg_ref, select_ref, slope_ref, ctx_ref,
        up_out, down_out, merge_out, heads_own, heads_other, lat_ref, sums_out, gm_out, adaln_out, context_out,
        x_up, y_up, x_down, y_down, x_merge, y_merge, y_heads, got_heads,
        share_u, got_u1, sum_u2, got_u2, sum_u3, got_u3, fin_u, swap_u, gots_u,
        send_d, keep_d, got_d1, sum_d2, got_d2, sum_d3, got_d3,
        send_m, keep_m, got_m1, sum_m2, got_m2, sum_m3, got_m3,
        got_h1, sum_h2, got_h2, sum_h3, got_h3, fin_h, swap_h, gots_h,
        weights, acc_ref, sum32, small, got_small, mod_rows, gm_ref, got_gm, ctx_acc,
        local_sem, sent_sem, came_sem
    ):
        row, col, img = lax.axis_index("row"), lax.axis_index("col"), lax.axis_index("img")
        x_me, y_me, c_me = img >> top & 1, col >> 1 & 1, col & 1
        zl, zh = row & 1, row >> 1 & 1
        to_x, to_y, to_c = {"img": img ^ 1 << top}, {"col": col ^ 2}, {"col": col ^ 1}
        to_z, to_far = {"row": row ^ 1}, {"row": row ^ 2}
        counts = {"local": 0, "remote": 0}
        remotes = []

        def local_copy(source, target):
            index = counts["local"]
            counts["local"] += 1
            made = pltpu.make_async_copy(source, target, local_sem.at[index])
            made.start()
            return made

        def send(source, target, device):
            index = counts["remote"]
            counts["remote"] += 1
            made = pltpu.make_async_remote_copy(
                src_ref=source, dst_ref=target, send_sem=sent_sem.at[index], recv_sem=came_sem.at[index],
                device_id=device, device_id_type=pl.DeviceIdType.MESH,
            )
            made.start()
            remotes.append(made)
            return made

        def strip(ref, start, size, unit):
            return ref.at[pl.ds(pl.multiple_of(start, unit), size)]

        def lanes(ref, source):
            return ref.at[..., pl.ds(source * tokens, tokens)]

        barrier = pltpu.get_barrier_semaphore()
        for device in (to_x, to_y, to_c, to_z, to_far):
            pl.semaphore_signal(barrier, inc=1, device_id=device, device_id_type=pl.DeviceIdType.MESH)
        pl.semaphore_wait(barrier, 5)

        y_mine = pl.ds(pl.multiple_of(y_me * block, block), block)
        y_other = pl.ds(pl.multiple_of((1 - y_me) * block, block), block)

        other_c = 1 - c_me
        y_heads[quarter:] = jnp.zeros((padded - quarter, all_tokens), BF16)
        heads_x = send(strip(triple_ref, (1 - x_me) * half_heads, half_heads, 576), got_heads, to_x)
        weights_in = local_copy(hw_ref, weights)
        up_waits, down_waits, merge_waits = [], [], []

        def upper_quarter(which):
            return strip(gup_ref, x_me * half_hidden + which * width, width, width)

        def came_quarter(which):
            return strip(gotu_y, which * width, width, width)

        up_waits += [
            send(in_ref, lanes(x_up, 2), to_c),
            send(upper_quarter(other_c), lanes(y_up, 2), to_c),
            send(gotu_x, lanes(x_up, 3), to_c),
            send(came_quarter(other_c), lanes(y_up, 3), to_c),
        ]
        up_local = [
            local_copy(in_ref, lanes(x_up, 0)),
            local_copy(gotu_x, lanes(x_up, 1)),
            local_copy(upper_quarter(c_me), lanes(y_up, 0)),
            local_copy(came_quarter(c_me), lanes(y_up, 1)),
        ]

        def gelu_rows(z, which):
            return strip(gel_ref, z * width + y_me * half + which * wide, wide, wide)

        def came_rows(z, which):
            return strip(gotd_x, z * half + which * wide, wide, wide)

        down_local = []
        for z in range(4):
            down_waits.append(send(gelu_rows(z, other_c), lanes(x_down.at[z], 2), to_c))
            down_waits.append(send(came_rows(z, other_c), lanes(x_down.at[z], 3), to_c))
            down_local.append(local_copy(gelu_rows(z, c_me), lanes(x_down.at[z], 0)))
            down_local.append(local_copy(came_rows(z, c_me), lanes(x_down.at[z], 1)))
        down_waits.append(send(gbb_ref, lanes(y_down, 2), to_c))
        down_waits.append(send(gotd_y, lanes(y_down, 3), to_c))
        down_local.append(local_copy(gbb_ref, lanes(y_down, 0)))
        down_local.append(local_copy(gotd_y, lanes(y_down, 1)))
        merge_local = []
        for z in range(4):
            merge_waits.append(
                send(att_ref.at[4 * z + 2 * y_me + other_c], lanes(x_merge.at[z], 2), to_c)
            )
            merge_waits.append(send(gotm_x.at[2 * z + other_c], lanes(x_merge.at[z], 3), to_c))
            merge_local.append(
                local_copy(att_ref.at[4 * z + 2 * y_me + c_me], lanes(x_merge.at[z], 0))
            )
            merge_local.append(local_copy(gotm_x.at[2 * z + c_me], lanes(x_merge.at[z], 1)))
        merge_waits.append(send(gba_ref, lanes(y_merge, 2), to_c))
        merge_waits.append(send(gotm_y, lanes(y_merge, 3), to_c))
        merge_local.append(local_copy(gba_ref, lanes(y_merge, 0)))
        merge_local.append(local_copy(gotm_y, lanes(y_merge, 1)))

        def triple_quarter(which):
            return strip(triple_ref, x_me * half_heads + which * quarter, quarter, 288)

        heads_c = [send(triple_quarter(other_c), lanes(y_heads.at[pl.ds(0, quarter)], 2), to_c)]
        heads_local = [local_copy(triple_quarter(c_me), lanes(y_heads.at[pl.ds(0, quarter)], 0))]

        def settle(local, came):
            for made in local:
                made.wait()
            for made in came:
                made.wait_recv()

        weights_in.wait()
        acc_ref[...] = jnp.zeros_like(acc_ref)
        tile = 384
        ones = jnp.ones((8, tokens), BF16)

        def entry_grad(t, carry):
            at = pl.multiple_of(t * tile, tile)
            acc_ref[...] += dot(weights[:, pl.ds(at, tile)], triple_ref[pl.ds(at, tile)])
            return carry

        lax.fori_loop(0, 5, entry_grad, 0)

        settle(up_local, up_waits)
        up_1 = []
        for start, size in up_cuts:
            def product(z, carry, start=start, size=size):
                at = pl.multiple_of(z * 2 * block, 2 * block)
                out = bf(dot(x_up[pl.ds(at, 2 * block)], y_up[start : start + size], 1, 1))
                share_u[z, :, start : start + size] = out
                return carry

            lax.fori_loop(0, 4, product, 0)
            cut = pl.ds(start, size)
            up_1.append(send(share_u.at[:, y_other, cut], got_u1.at[:, :, cut], to_y))

        x_heads = x_up
        heads_in = local_copy(xh_in, x_heads)

        settle(down_local, down_waits)
        down_1 = []
        there = pl.multiple_of((1 - x_me) * half, half)
        here = pl.multiple_of(x_me * half, half)
        for z in range(4):
            send_d[z] = bf(dot(x_down[z], y_down[pl.ds(there, half)], 1, 1))
        for start, size in down_cuts:
            cut = pl.ds(start, size)
            down_1.append(send(send_d.at[:, cut], got_d1.at[:, cut], to_x))
        for z in range(4):
            keep_d[z] = bf(dot(x_down[z], y_down[pl.ds(here, half)], 1, 1))

        settle(merge_local, merge_waits)
        for z in range(4):
            send_m[z] = bf(dot(x_merge[z], y_merge[pl.ds(there, half)], 1, 1))
        merge_1 = send(send_m, got_m1, to_x)
        for z in range(4):
            keep_m[z] = bf(dot(x_merge[z], y_merge[pl.ds(here, half)], 1, 1))

        heads_x.wait_recv()

        def got_quarter(which):
            return strip(got_heads, which * quarter, quarter, 288)

        heads_c.append(send(got_quarter(other_c), lanes(y_heads.at[pl.ds(0, quarter)], 3), to_c))
        heads_local.append(local_copy(got_quarter(c_me), lanes(y_heads.at[pl.ds(0, quarter)], 1)))

        lax.fori_loop(5, 3 * width // tile, entry_grad, 0)
        next_weights = local_copy(aw_ref.at[:, pl.ds(0, 3 * width)], weights)
        grad_in = acc_ref[...].T
        normed, rstd = normalize(emb_ref[...])
        grad = gres_ref[...] + norm_pull(normed, rstd, grad_in * (1.0 + rows_ref[1:2, :]))
        grad_low = bf(grad)
        lat_ref[...] = dot(grad_low, pw_ref[...], 1, 1)
        sum32[...] = jnp.zeros_like(sum32)
        sum32[0:pixels_count] = fwg_ref[...]
        base = pixels_count
        for k in range(hidden // width):
            sum32[base + k : base + k + 1] = ubg_ref[:, k * width : (k + 1) * width]
        base += hidden // width
        sum32[base : base + 1] = rsum_ref[5:6]
        sum32[base + 1 : base + 2] = rsum_ref[4:5]
        sum32[base + 2 : base + 3, 0:pixels_count] = fbg_ref[...]
        base += 3
        sum32[base : base + pixels_count] = dot(pat_ref[...], grad_low, 0, 0)
        base += pixels_count
        sum32[base : base + 1] = column_sum(grad)
        sum32[base + 1 : base + 2] = dot(ones, triple_ref[0:width], 1, 1)[0:1]
        sum32[base + 2 : base + 3] = dot(ones, triple_ref[2 * width : 3 * width], 1, 1)[0:1]
        colsum_at = 48
        small[0] = bf(sum32[...])
        mine = row * 4 + col
        mod_rows[mine, 0:1] = column_sum(grad_in)
        mod_rows[mine, 1:2] = column_sum(grad_in * normed)
        mod_rows[mine, 2:6] = rsum_ref[0:4]
        mod_rows[mine, 6:8] = jnp.zeros((2, width), F32)

        levels = ((to_c, 0), (to_y, 1), (to_z, 2), (to_far, 3))
        state = {"level": 0}

        def small_send():
            device, level = levels[state["level"]]
            first = mine >> level << level
            span = pl.ds(first, 1 << level)
            state["copies"] = [
                send(small.at[level], got_small.at[level], device),
                send(mod_rows.at[span], mod_rows.at[span], device),
            ]

        def small_step():
            for made in state["copies"]:
                made.wait_recv()
            level = state["level"]
            small[level + 1] = bf(small[level].astype(F32) + got_small[level].astype(F32))
            state["level"] += 1
            if state["level"] < len(levels):
                small_send()

        small_send()

        share_h = x_down
        heads_in.wait()
        settle(heads_local, heads_c)
        heads_1 = []
        for start, size in head_cuts:
            def product(z, carry, start=start, size=size):
                at = pl.multiple_of(z * 2 * block, 2 * block)
                out = bf(dot(x_heads[pl.ds(at, 2 * block)], y_heads[start : start + size], 1, 1))
                share_h[z, :, start : start + size] = out
                return carry

            lax.fori_loop(0, 4, product, 0)
            cut = pl.ds(start, size)
            heads_1.append(send(share_h.at[:, y_other, cut], got_h1.at[:, :, cut], to_y))

        def add(one, two):
            return bf(one.astype(F32) + two.astype(F32))

        def columns_second(waits, k, cuts, share, got, total, target):
            start, size = cuts[k]
            cut = pl.ds(start, size)
            waits[k].wait_recv()
            total[:, :, :, cut] = add(share[:, y_mine, cut], got[:, :, cut]).reshape(2, 2, block, size)
            return send(total.at[:, 1 - zl, :, cut], target.at[:, :, cut], to_z)

        def columns_third(wait, k, cuts, share, got, total, target):
            start, size = cuts[k]
            cut = pl.ds(start, size)
            wait.wait_recv()
            total[:, :, cut] = add(share[:, zl, :, cut], got[:, :, cut])
            return send(total.at[1 - zh, :, cut], target.at[:, cut], to_far)

        def columns_last(wait, k, cuts, share, got, final):
            start, size = cuts[k]
            cut = pl.ds(start, size)
            wait.wait_recv()
            final[:, cut] = share[zh, :, cut].astype(F32) + got[:, cut].astype(F32)

        def rows_second(wait, start, size, kept, got, total, target):
            cut = pl.ds(start, size)
            wait.wait_recv()
            total[:, :, cut] = add(kept[:, cut], got[:, cut]).reshape(2, 2, size, half)
            return send(total.at[:, 1 - zl, cut], target.at[:, cut], to_z)

        def rows_third(wait, start, size, share, got, total, target):
            cut = pl.ds(start, size)
            wait.wait_recv()
            total[:, cut] = add(share[:, zl, cut], got[:, cut])
            return send(total.at[1 - zh, cut], target.at[cut], to_far)

        def rows_last(wait, start, size, share, got, out):
            cut = pl.ds(start, size)
            wait.wait_recv()
            out[cut] = share[zh, cut].astype(F32) + got[cut].astype(F32)

        up_2, up_3, heads_2, heads_3 = [], [], [], []
        down_2, down_3 = [], []
        up_2.append(columns_second(up_1, 0, up_cuts, share_u, got_u1, sum_u2, got_u2))
        small_step()
        up_2.append(columns_second(up_1, 1, up_cuts, share_u, got_u1, sum_u2, got_u2))
        up_3.append(columns_third(up_2[0], 0, up_cuts, sum_u2, got_u2, sum_u3, got_u3))
        small_step()
        up_2.append(columns_second(up_1, 2, up_cuts, share_u, got_u1, sum_u2, got_u2))
        up_3.append(columns_third(up_2[1], 1, up_cuts, sum_u2, got_u2, sum_u3, got_u3))
        down_2.append(rows_second(down_1[0], *down_cuts[0], keep_d, got_d1, sum_d2, got_d2))
        small_step()
        heads_2.append(columns_second(heads_1, 0, head_cuts, share_h, got_h1, sum_h2, got_h2))
        down_2.append(rows_second(down_1[1], *down_cuts[1], keep_d, got_d1, sum_d2, got_d2))
        up_3.append(columns_third(up_2[2], 2, up_cuts, sum_u2, got_u2, sum_u3, got_u3))
        down_3.append(rows_third(down_2[0], *down_cuts[0], sum_d2, got_d2, sum_d3, got_d3))
        small_step()

        for j in range(6):
            rows_j = bf(mod_rows[:, j, :])
            gm = bf(dot(select_ref[...], rows_j))
            gm_ref[:, j * width : (j + 1) * width] = gm
            small[4, colsum_at + j : colsum_at + j + 1] = bf(column_sum(gm.astype(F32)))
        if images == 2:
            away = pl.ds(pl.multiple_of((1 - x_me) * 3 * width, width), 3 * width)
            last_copies = [
                send(small.at[4], got_small.at[4], to_x),
                send(gm_ref.at[:, away], got_gm, to_x),
            ]
        merge_2 = rows_second(merge_1, 0, head, keep_m, got_m1, sum_m2, got_m2)
        down_2.append(rows_second(down_1[2], *down_cuts[2], keep_d, got_d1, sum_d2, got_d2))
        heads_2.append(columns_second(heads_1, 1, head_cuts, share_h, got_h1, sum_h2, got_h2))
        heads_3.append(columns_third(heads_2[0], 0, head_cuts, sum_h2, got_h2, sum_h3, got_h3))
        down_3.append(rows_third(down_2[1], *down_cuts[1], sum_d2, got_d2, sum_d3, got_d3))

        ctx_acc[...] = jnp.zeros_like(ctx_acc)

        def context_part(first):
            for j in range(3):
                at = slice((first + j) * width, (first + j + 1) * width)
                ctx_acc[...] += dot(gm_ref[:, at], weights[:, j * width : (j + 1) * width], 1, 1)

        next_weights.wait()
        context_part(0)
        next_weights = local_copy(aw_ref.at[:, pl.ds(3 * width, 3 * width)], weights)

        for k in range(len(up_cuts)):
            columns_last(up_3[k], k, up_cuts, sum_u3, got_u3, fin_u)
        swap_u[...] = bf(fin_u[pl.ds(pl.multiple_of(other_c * head, 8), head)])
        up_swap = send(swap_u, gots_u, to_c)
        merge_3 = rows_third(merge_2, 0, head, sum_m2, got_m2, sum_m3, got_m3)
        down_3.append(rows_third(down_2[2], *down_cuts[2], sum_d2, got_d2, sum_d3, got_d3))
        heads_3.append(columns_third(heads_2[1], 1, head_cuts, sum_h2, got_h2, sum_h3, got_h3))
        next_weights.wait()
        context_part(3)
        context_out[...] = ctx_acc[...] * slope_ref[...]
        if images == 2:
            for made in last_copies:
                made.wait_recv()
            small[5] = bf(small[4].astype(F32) + got_small[4].astype(F32))
            home = pl.ds(pl.multiple_of(x_me * 3 * width, width), 3 * width)
            adaln_out[...] = dot(ctx_ref[0], gm_ref[:, home], 0, 0) + dot(ctx_ref[1], got_gm[...], 0, 0)
            sums_out[...] = small[5].astype(F32)
        else:
            sums_out[...] = small[4].astype(F32)
            adaln_out[...] = jnp.zeros_like(adaln_out)
        gm_out[...] = gm_ref[...]
        up_swap.wait_recv()
        mine_at = pl.ds(pl.multiple_of(c_me * width, width), width)
        other_at = pl.ds(pl.multiple_of(other_c * width, width), width)
        up_out[:, mine_at] = fin_u[pl.ds(pl.multiple_of(c_me * head, 8), head)]
        up_out[:, other_at] = gots_u[...].astype(F32)
        for k in range(len(down_cuts)):
            rows_last(down_3[k], *down_cuts[k], sum_d3, got_d3, down_out)
        rows_last(merge_3, 0, head, sum_m3, got_m3, merge_out)
        for k in range(len(head_cuts)):
            columns_last(heads_3[k], k, head_cuts, sum_h3, got_h3, fin_h)
        swap_h[...] = bf(fin_h[pl.ds(pl.multiple_of(other_c * head, 8), head)])
        heads_swap = send(swap_h, gots_h, to_c)
        heads_own[...] = fin_h[pl.ds(pl.multiple_of(c_me * head, 8), head)][:, :quarter]
        heads_swap.wait_recv()
        heads_other[...] = gots_h[...].astype(F32)[:, :quarter]
        for made in remotes:
            made.wait_send()

    vmem = pl.BlockSpec(memory_space=pltpu.VMEM)
    anywhere = pl.BlockSpec(memory_space=pl.ANY)
    dma = pltpu.SemaphoreType.DMA
    buf = lambda *shape: pltpu.VMEM(shape, BF16)
    buf32 = lambda *shape: pltpu.VMEM(shape, F32)
    out = lambda *shape: jax.ShapeDtypeStruct(shape, F32)
    return pl.pallas_call(
        kernel,
        in_specs=[anywhere] * 13 + [vmem] + [anywhere] * 2 + [vmem] * 12,
        out_specs=[vmem] * 10,
        out_shape=[
            out(head, half_hidden), out(wide, half), out(head, half), out(head, quarter), out(head, quarter),
            out(tokens, pixels_count), out(SUMS, width),
            jax.ShapeDtypeStruct((SLOT_ROWS, 6 * width), BF16),
            out(head, 3 * width), out(SLOT_ROWS, width),
        ],
        scratch_shapes=[
            buf(width, all_tokens), buf(width, all_tokens),
            buf(4, wide, all_tokens), buf(width, all_tokens),
            buf(4, head, all_tokens), buf(width, all_tokens),
            buf(padded, all_tokens), buf(half_heads, tokens),
            buf(4, 2 * block, width), buf(4, block, width), buf(2, 2, block, width), buf(2, block, width),
            buf(2, block, width), buf(block, width), buf32(block, width), buf(head, width), buf(head, width),
            buf(4, wide, half), buf(4, wide, half), buf(4, wide, half), buf(2, 2, wide, half),
            buf(2, wide, half), buf(2, wide, half), buf(wide, half),
            buf(4, head, half), buf(4, head, half), buf(4, head, half), buf(2, 2, head, half),
            buf(2, head, half), buf(2, head, half), buf(head, half),
            buf(4, block, padded), buf(2, 2, block, padded),
            buf(2, block, padded), buf(2, block, padded), buf(block, padded), buf32(block, padded),
            buf(head, padded), buf(head, padded),
            buf(width, 3 * width), buf32(width, tokens), buf32(SUMS, width), buf(6, SUMS, width),
            buf(5, SUMS, width), buf32(16, 8, width), buf(SLOT_ROWS, 6 * width), buf(SLOT_ROWS, 3 * width),
            buf32(SLOT_ROWS, width),
            dma((40,)), dma((80,)), dma((80,)),
        ],
        compiler_params=pltpu.CompilerParams(
            vmem_limit_bytes=VMEM_LIMIT, collective_id=1, has_side_effects=True
        ),
        cost_estimate=cost(2 * 4 * tokens * width * (hidden + width), 60 * 1024 * 1024),
        name="tail",
    )(
        mlp_in, upper_t, gelu_t, branch_t, attended_h, merge_t, got_up, got_up_y, got_down, got_down_y, got_att,
        got_merge, entry_heads, triple, heads_weight, adaln_weight, embedded, grad_resid, patches,
        patch_weight, rows_a, final_grad, up_sums, rows_sums, final_bias_grad, select, silu_slope, context_rows
    )


def beside(*parts):
    return jnp.concatenate(parts, axis=1)


def above(*parts):
    return jnp.concatenate(parts, axis=0)


def rest_of_img(array):
    for level in reversed(range(lax.axis_size("img").bit_length() - 2)):
        mine = bit_of("img", level)
        got = swap(bf(half_of(array, 1 - mine, 1)), "img", level)
        array = half_of(array, mine, 1).astype(F32) + got.astype(F32)
    return array


def gather_all(array, axis):
    for level in range(lax.axis_size(axis).bit_length() - 1):
        high = bit_of(axis, level) == 1
        other = swap(array, axis, level)
        array = jnp.where(
            high, jnp.concatenate([other, array], axis=0), jnp.concatenate([array, other], axis=0)
        )
    return array


def shifted(array, axes, by):
    sizes = [lax.axis_size(axis) for axis in axes]
    pairs = []
    total = math.prod(sizes)
    for index in range(total):
        rest, target, scale = index, 0, 1
        for size, step in reversed(list(zip(sizes, by))):
            target += (rest % size + step) % size * scale
            rest //= size
            scale *= size
        pairs.append((index, target))
    return lax.ppermute(array, axes, pairs)


def roll_in(tile):
    above = shifted(tile[:, -1:, :-1], ("row",), (1,))
    left = shifted(tile[:, :-1, -1:], ("col",), (1,))
    corner = shifted(tile[:, -1:, -1:], ("row", "col"), (1, 1))
    first = jnp.concatenate([corner, above], axis=2)
    rest = jnp.concatenate([left, tile[:, :-1, :-1]], axis=2)
    return jnp.concatenate([first, rest], axis=1)


def roll_out(tile):
    below = shifted(tile[:, :1, 1:], ("row",), (-1,))
    right = shifted(tile[:, 1:, :1], ("col",), (-1,))
    corner = shifted(tile[:, :1, :1], ("row", "col"), (-1, -1))
    last = jnp.concatenate([below, corner], axis=2)
    rest = jnp.concatenate([tile[:, 1:, 1:], right], axis=2)
    return jnp.concatenate([rest, last], axis=1)


def to_tokens(tile_data):
    channels, height, breadth = tile_data.shape
    return (
        tile_data.reshape(channels, height // 2, 2, breadth // 2, 2)
        .transpose(1, 3, 0, 2, 4)
        .reshape(height * breadth // 4, channels * 4)
    )


def to_tile(tokens, channels, height, breadth):
    return (
        tokens.reshape(height // 2, breadth // 2, channels, 2, 2)
        .transpose(2, 0, 3, 1, 4)
        .reshape(channels, height, breadth)
    )


def wave_table(index, quarter):
    frequency = 1.0 / 10000.0 ** (jnp.arange(quarter, dtype=F32) / quarter)
    angle = index.astype(F32)[:, None] * frequency[None, :]
    return jnp.concatenate([jnp.sin(angle), jnp.cos(angle)], axis=1)


def local(
    latent, context, segment, patch_weight, patch_bias, adaln_weight, adaln_bias, heads_weight,
    query_bias, value_bias, merge_weight, merge_bias, up_weight, up_bias, down_weight, down_bias,
    final_weight, final_bias, cotangent
):
    rows_count, cols_count = lax.axis_size("row"), lax.axis_size("col")
    row_index, col_index = lax.axis_index("row"), lax.axis_index("col")
    channels, height, breadth = latent.shape[1:]
    tile_rows, tile_cols = height // 2, breadth // 2
    assert tile_rows == BLOCK // 2 and tile_cols == BLOCK // 2
    assert rows_count == 4 and cols_count == 4
    tokens = tile_rows * tile_cols
    width = patch_weight.shape[1]
    head = width // HEADS
    scale = 1.0 / math.sqrt(head)
    slots = context.shape[0]

    ids = segment[0, ::tile_rows, ::tile_cols]
    slot = ids[row_index, col_index]
    partners = [
        ids[row_index ^ dz, col_index ^ dc] for dz, dc in ((0, 0), (0, 1), (1, 0), (1, 1))
    ]
    tile_bias = jnp.where(jnp.stack(partners) == slot, 0.0, MASKED).astype(F32)
    live = (slot >= 0).astype(F32)[None]
    is_large = slot % 5 == 4

    context_f = context.astype(F32)
    silu_out, silu_pull = jax.vjp(jax.nn.silu, context_f)
    context_low = bf(silu_out)
    row = lax.dynamic_slice_in_dim(context_low, jnp.maximum(slot, 0), 1, 0)
    row = jnp.broadcast_to(row, (16, width))
    adaln_bias2 = adaln_bias[None]
    mod_a = modulation_rows(row, live, adaln_weight, adaln_bias2, 0, 2 * width, 768)

    both = jnp.concatenate([latent[0], cotangent[0]], axis=0)
    both = roll_in(both)
    patches = to_tokens(both[:channels])
    cot = bf(to_tokens(both[channels:]).astype(F32) * live)
    grid_r = row_index * tile_rows + jnp.arange(tile_rows, dtype=jnp.int32)
    grid_c = col_index * tile_cols + jnp.arange(tile_cols, dtype=jnp.int32)
    wave_r = wave_table(jnp.where(is_large, grid_r % BLOCK, grid_r % (BLOCK // 2)), width // 4)
    wave_c = wave_table(jnp.where(is_large, grid_c % BLOCK, grid_c % (BLOCK // 2)), width // 4)
    half = width // 2
    base = jnp.concatenate(
        [
            jnp.broadcast_to(wave_r[:, None, :], (tile_rows, tile_cols, half)),
            jnp.broadcast_to(wave_c[None, :, :], (tile_rows, tile_cols, half)),
        ],
        axis=2,
    ).reshape(tokens, width) + patch_bias.astype(F32)

    bias3 = jnp.concatenate(
        [query_bias.astype(F32), jnp.zeros((width,), F32), value_bias.astype(F32)]
    )[None]
    shift_a, scale_a = mod_a[:, :width], mod_a[:, width:]
    embedded, attn_in, attn_in_t, pair_own = embed_project(
        patches, patch_weight, base, shift_a, scale_a, heads_weight, bias3, width, 2 * width, 384
    )
    pair_z = swap(pair_own, "row", 0)
    entry_heads = beside(attn_in_t, swap(attn_in_t, "img", lax.axis_size("img").bit_length() - 2))
    entry_heads = beside(entry_heads, swap(entry_heads, "col", 0))
    pair_c = swap(pair_own, "col", 0)
    queries = project(attn_in, heads_weight, bias3, 0, width, 384)
    mod_b = modulation_rows(row, live, adaln_weight, adaln_bias2, 2 * width, 4 * width, 768)
    rows_b = jnp.concatenate([mod_b[0:1].reshape(4, width), jnp.zeros((4, width), F32)], axis=0)
    pair_zc = swap(pair_z, "col", 0)
    by_head = lambda array: array.reshape(-1, head, tokens)
    queries_h = by_head(queries)
    pairs = [by_head(pair) for pair in (pair_own, pair_c, pair_z, pair_zc)]
    attended, lse = attention_forward(tile_bias, queries_h, pairs, scale, 2)
    attended_t = attended.reshape(width, tokens)
    (
        pixels, final_grad_t, sums_b, up_bias_grad, mlp_in_t, grad_branch_b_t, gelu_t, grad_upper_t,
        grad_branch_a_t, grad_resid_a, triple, got_up, got_up_y, got_down, got_down_y, got_att, got_merge
    ) = middle(
        live, tile_bias, attended_t, merge_weight, merge_bias[None], embedded, rows_b, up_weight,
        up_bias[None], down_weight, down_bias[None], cot, final_weight, final_bias[None], queries_h, pairs,
        lse, scale,
    )
    rows_a = jnp.concatenate([shift_a[0:1], scale_a[0:1], jnp.zeros((6, width), F32)], axis=0)
    final_bias_grad = jnp.sum(cot.astype(F32), axis=0, keepdims=True)
    hidden = up_weight.shape[1]
    features = patches.shape[1]
    images = lax.axis_size("img")
    flat_ids = ids.reshape(-1)
    select = (jnp.arange(SLOT_ROWS, dtype=jnp.int32)[:, None] == flat_ids[None, :]).astype(BF16)
    (silu_slope,) = silu_pull(jnp.ones_like(context_f))
    spare = ((0, SLOT_ROWS - slots), (0, 0))
    share = width // (rows_count * cols_count)
    flat = row_index * cols_count + col_index
    all_context = gather_all(context_low, "img")
    context_rows = lax.dynamic_slice_in_dim(all_context, flat * share, share, 1)
    by_canvas = context_rows.reshape(images, slots, share)
    own_rows = pick(by_canvas, lax.axis_index("img"), 0)
    next_rows = pick(by_canvas, lax.axis_index("img") ^ 1, 0)
    pair_rows = jnp.stack([jnp.pad(own_rows, spare), jnp.pad(next_rows, spare)])
    (
        up_weight_grad, down_weight_grad, merge_weight_grad, heads_own, heads_other, grad_patches, sums, grad_mod,
        adaln_weight_grad, context_gradient
    ) = tail(
        (mlp_in_t, grad_upper_t, gelu_t, grad_branch_b_t, attended, grad_branch_a_t), got_up, got_up_y,
        got_down, got_down_y, got_att.reshape(8, head, tokens), got_merge, entry_heads,
        triple.reshape(3 * width, tokens), heads_weight, adaln_weight, embedded, grad_resid_a, patches,
        patch_weight, rows_a, final_grad_t, up_bias_grad, sums_b, final_bias_grad, select,
        jnp.pad(silu_slope, spare), pair_rows,
    )
    up_weight_grad = rest_of_img(up_weight_grad)
    down_weight_grad = rest_of_img(down_weight_grad)
    merge_weight_grad = rest_of_img(merge_weight_grad)
    heads_weight_grad = rest_of_img(
        jnp.where(col_index & 1 == 1, beside(heads_other, heads_own), beside(heads_own, heads_other))
    )
    context_gradient = context_gradient[:slots]
    extra = features + hidden // width
    late = sums[extra + 3 :]
    if images == 2:
        adaln_bias_grad = sums[48:54].reshape(6 * width)
    else:
        for level in range(images.bit_length() - 1):
            sums = sums + swap(sums, "img", level)
        late = sums[extra + 3 :]
        all_mod = gather_all(grad_mod[:slots], "img")
        part = 6 * width // images
        mod_cols = lax.dynamic_slice_in_dim(all_mod, lax.axis_index("img") * part, part, 1)
        adaln_weight_grad = dot(context_rows, mod_cols, 0, 0)
        adaln_bias_grad = jnp.sum(all_mod.astype(F32), axis=0)

    tiles_out = jnp.concatenate(
        [
            to_tile(pixels, channels, height, breadth),
            to_tile(grad_patches, channels, height, breadth),
        ],
        axis=0,
    )
    rolled = roll_out(tiles_out)

    return (
        rolled[:channels][None],
        rolled[channels:][None],
        context_gradient,
        late[:features],
        late[features],
        adaln_weight_grad,
        adaln_bias_grad,
        heads_weight_grad,
        late[features + 1],
        late[features + 2],
        merge_weight_grad,
        sums[extra + 1],
        up_weight_grad,
        sums[features:extra].reshape(hidden),
        down_weight_grad,
        sums[extra],
        sums[:features].T,
        sums[extra + 2, :features],
    )


def solution(mesh):
    tile = P("img", None, "row", "col")
    share = P(("row", "col"), "img")
    none = P()
    in_specs = (tile, P("img", None), P("img", None, None)) + (none,) * 15 + (tile,)
    out_specs = (
        tile, tile, P("img", None), none, none, share, none, share, none, none, share, none, share,
        none, share, none, none, none
    )
    return jax.shard_map(local, mesh=mesh, in_specs=in_specs, out_specs=out_specs, check_vma=False)
```
